512 devices in a mesh: dp: 64 (over z_lo, x, core), tensor: 8 (over y, z_hi).
Axes of the slice: x: 4, y: 4, z: 16 (z_hi: 2, z_lo: 8; z = z_hi * 8 + z_lo), core: 2. Of those that a mesh axis runs over, the one named last changes fastest.
Arguments:
- o_inputs: bfloat16 [16384, 8192], P('dp', 'tensor'), may hold values from -6 to 6
- o_gradients: bfloat16 [16384, 8192], P('dp', 'tensor'), may hold values from -6 to 6
- up_inputs: bfloat16 [16384, 8192], P('dp', 'tensor'), may hold values from -6 to 6
- up_gradients: bfloat16 [16384, 28672], P('dp', 'tensor'), may hold values from -6 to 6
- o_in_proj: bfloat16 [8192, 32], P('tensor'), may hold values from -0.0625 to 0.0625
- o_out_proj: bfloat16 [8192, 32], P('tensor'), may hold values from -0.0625 to 0.0625
- up_in_proj: bfloat16 [8192, 32], P('tensor'), may hold values from -0.0625 to 0.0625
- up_out_proj: bfloat16 [28672, 32], P('tensor'), may hold values from -0.03125 to 0.03125
- segment_ids: int32 [64, 256], P('dp'), may hold values from 0 to 3, never falling along the last dimension, each value on 1 to 128 neighbouring positions
- owner_map: int32 [64], replicated, may hold values from 0 to 63, each once
Outputs:
- example_vectors: float32 [2, 256, 1024], P(None, 'dp', 'tensor')
- fisher_owned: float32 [64, 32, 1024], P('dp', None, 'tensor')
The draws below stay inside these ranges and needn't reach their ends.
Inputs may be any that keep to these rules, and one draw needn't show every extreme that they name: `segment_ids`: within each row, ids never fall; each of the 4 ids holds 1 to 128 tokens, and one holds exactly that many. `owner_map`: each block index appears exactly once.
All inputs are finite; a program needn't handle non-finite values.
Results may differ from the reference program's by a relative error of at most 0.0003.
Values sent between devices are 32-bit elements; how exact they have to be, the bound alone decides.
A program may use at most 64 MiB of HBM per device.

```python
import math
import jax
import jax.numpy as jnp
import numpy as np
from jax import lax

D = 8192
FF = 28672
KIN = 32
KOUT = 32
KK = 1024
TOK_DEV = 256
EX_DEV = 4
BLOCKS = 64
TOKENS = 16384
EXAMPLES = 256
OWN_ROWS = 32
N_DP = 64


def level_of(stream_key, dims, cuts, low, top_value):
    loudness, own = 1.0, jax.random.fold_in(stream_key, 6)
    for axis_at, parts in cuts:
        steps = jnp.exp(jax.random.uniform(jax.random.fold_in(own, axis_at), (parts,), jnp.float32, low / len(cuts), top_value / len(cuts)))
        loudness = loudness * jnp.repeat(steps, dims[axis_at] // parts).reshape([-1 if axis == axis_at else 1 for axis in range(len(dims))])
    return loudness


def length_profile(number_of, total, reach, lean):
    loads = [(1 << 20) // math.isqrt(grade ** lean) + 1 for grade in range(2, number_of + 1)]
    surplus, holding = total - reach - (number_of - 1), [1] * (number_of - 1)
    while surplus > 0:
        free = [i for i in range(number_of - 1) if holding[i] < reach]
        whole, budget = sum([loads[i] for i in free]), surplus
        for i in free:
            extra = min(reach - holding[i], max(1, budget * loads[i] // whole), surplus)
            holding[i] = holding[i] + extra
            surplus = surplus - extra
    return np.array([reach] + holding)


def uneven(rng, count, total, limit, lean):
    if count == 2:
        one = jax.random.randint(rng, (), max(1, total - limit), min(limit, total - 1) + 1)
        return jnp.stack([one, total - one])
    lengths = jnp.asarray(length_profile(count, total, limit, lean), jnp.int32)
    pairs = (count - 1) // 2
    donor, sink = lengths[1:1 + 2 * pairs:2], lengths[2:2 + 2 * pairs:2]
    room = jnp.minimum(donor - 1, limit - sink)
    passed = jax.random.randint(jax.random.fold_in(rng, 1), (pairs,), 0, 1 << 20) % (room + 1)
    lengths = lengths.at[1:1 + 2 * pairs:2].set(donor - passed).at[2:2 + 2 * pairs:2].set(sink + passed)
    return lengths[jax.random.permutation(jax.random.fold_in(rng, 2), count)]


def bell_draw(own_key, shape, scale, most, split=(), kind=jnp.bfloat16):
    drawn = scale * jax.random.normal(own_key, shape, jnp.float32)
    if split:
        drawn = drawn * level_of(own_key, shape, split, -0.22, 0.18)
    return jnp.clip(drawn, -most, most).astype(kind)


def setup_inputs(seed: int = 0) -> dict:
    key_list = jax.random.split(jax.random.key(seed), 11)
    o_inputs = bell_draw(key_list[0], (TOKENS, D), 1.0, 6.0, ((0, 64), (1, 8)))
    o_gradients = bell_draw(key_list[1], (TOKENS, D), 1.0, 6.0, ((0, 64), (1, 8)))
    up_inputs = bell_draw(key_list[2], (TOKENS, D), 1.0, 6.0, ((0, 64), (1, 8)))
    up_gradients = bell_draw(key_list[3], (TOKENS, FF), 1.0, 6.0, ((0, 64), (1, 8)))
    o_in_proj = bell_draw(key_list[4], (D, KIN), D ** -0.5, 0.0625, ((0, 8),))
    o_out_proj = bell_draw(key_list[5], (D, KOUT), D ** -0.5, 0.0625, ((0, 8),))
    up_in_proj = bell_draw(key_list[6], (D, KIN), D ** -0.5, 0.0625, ((0, 8),))
    up_out_proj = bell_draw(key_list[7], (FF, KOUT), FF ** -0.5, 0.03125, ((0, 8),))
    segment_ids = jax.vmap(lambda own: jnp.searchsorted(jnp.cumsum(uneven(own, EX_DEV, TOK_DEV, TOK_DEV // 2, 2)), jnp.arange(TOK_DEV), side="right"))(jax.random.split(key_list[8], BLOCKS)).reshape((BLOCKS, TOK_DEV)).astype(jnp.int32)
    owner_map = jax.random.permutation(key_list[9], BLOCKS).astype(jnp.int32)
    return dict(o_inputs=o_inputs, o_gradients=o_gradients, up_inputs=up_inputs, up_gradients=up_gradients, o_in_proj=o_in_proj, o_out_proj=o_out_proj, up_in_proj=up_in_proj, up_out_proj=up_out_proj, segment_ids=segment_ids, owner_map=owner_map)


def vectors(inputs, gradients, in_proj, out_proj, segment_ids):
    in_low = jnp.dot(inputs, in_proj, preferred_element_type=jnp.float32)
    out_low = jnp.dot(gradients, out_proj, preferred_element_type=jnp.float32)
    outers = (out_low[:, :, None] * in_low[:, None, :]).reshape(N_DP, TOK_DEV, KK)
    onehot = (segment_ids[:, :, None] == jnp.arange(EX_DEV, dtype=jnp.int32)[None, None, :]).astype(jnp.float32)
    summed = jnp.einsum("gte,gtk->gek", onehot, outers, precision=lax.Precision.HIGHEST)
    vector_scale = (EX_DEV / TOK_DEV) ** 0.5
    return (summed * vector_scale).reshape(EXAMPLES, KK)


def reference(o_inputs, o_gradients, up_inputs, up_gradients, o_in_proj, o_out_proj, up_in_proj, up_out_proj, segment_ids, owner_map):
    vector_o = vectors(o_inputs, o_gradients, o_in_proj, o_out_proj, segment_ids)
    vector_up = vectors(up_inputs, up_gradients, up_in_proj, up_out_proj, segment_ids)
    example_vectors = jnp.stack([vector_o, vector_up])
    fisher_o = jnp.dot(vector_o.T, vector_o, precision=lax.Precision.HIGHEST) / EXAMPLES
    fisher_up = jnp.dot(vector_up.T, vector_up, precision=lax.Precision.HIGHEST) / EXAMPLES
    stacked = jnp.concatenate([fisher_o, fisher_up], axis=0)
    fisher_owned = stacked.reshape(N_DP, OWN_ROWS, KK)[owner_map]
    return example_vectors, fisher_owned
```

```python
import functools

import jax
import jax.numpy as jnp
from jax import lax
from jax.experimental import pallas as pl
from jax.experimental.pallas import tpu as pltpu
from jax.sharding import PartitionSpec as P

TOK = 256
EX = 4
KP = 32
BLOCKS = 64
EXAMPLES = 256
YN = 4
HIGH = lax.Precision.HIGHEST
MESH = pl.DeviceIdType.MESH
NT = (((1,), (1,)), ((), ()))
TN = (((0,), (0,)), ((), ()))


def kernel(
    n_dp,
    xo_ref, go_ref, xu_ref, gu_ref, pxo_ref, pgo_ref, pxu_ref, pgu_ref, seg_ref, own_ref,
    ev_ref, f_ref,
    xo, go, xu, gu, pxo, pgo, pxu, pgu, seg_v, own_v, ev, f_v,
    part, recv_y, recv_z, sum_z, full, g_ref, v_ref, send_d, recv_d,
    in_sem, out_sem, sy_sem, ry_sem, sz_sem, rz_sem, sg_sem, rg_sem, sd_sem, rd_sem,
):
    d = lax.axis_index("dp")
    t = lax.axis_index("tensor")
    y, zh = t // 2, lax.rem(t, 2)
    partner = y * 2 + (1 - zh)

    def y_peer(j):
        return lax.rem(y + j, YN)

    half = TOK // 2
    loads = [
        (pxo_ref, pxo), (xo_ref, xo), (pgo_ref, pgo), (go_ref, go), (pxu_ref, pxu), (xu_ref, xu), (pgu_ref, pgu),
        (gu_ref.at[pl.ds(0, half)], gu.at[pl.ds(0, half)]), (gu_ref.at[pl.ds(half, half)], gu.at[pl.ds(half, half)]),
        (seg_ref, seg_v), (own_ref, own_v),
    ]
    copies = [pltpu.make_async_copy(s, dst, in_sem.at[i]) for i, (s, dst) in enumerate(loads)]
    for c in copies:
        c.start()

    barrier = pltpu.get_barrier_semaphore()
    for j in range(1, YN):
        pl.semaphore_signal(barrier, inc=1, device_id={"tensor": y_peer(j) * 2 + zh}, device_id_type=MESH)
    pl.semaphore_signal(barrier, inc=1, device_id={"tensor": partner}, device_id_type=MESH)

    def greet(k, carry):
        pl.semaphore_signal(barrier, inc=1, device_id={"dp": lax.rem(d + k, n_dp)}, device_id_type=MESH)
        return carry

    lax.fori_loop(1, n_dp, greet, 0)

    def project(w, x):
        return lax.dot_general(w, x, NT, preferred_element_type=jnp.float32)

    def y_send(i):
        return pltpu.make_async_remote_copy(
            src_ref=part.at[i], dst_ref=recv_y.at[y], send_sem=sy_sem.at[i], recv_sem=ry_sem.at[y],
            device_id={"tensor": i * 2 + zh}, device_id_type=MESH,
        )

    for i, (w, x) in enumerate(((pxo, xo), (pgo, go), (pxu, xu), (pgu, gu))):
        copies[2 * i].wait()
        copies[2 * i + 1].wait()
        if i < 3:
            part[i] = project(w[...], x[...])
        else:
            part[i, :, pl.ds(0, half)] = project(w[...], x[pl.ds(0, half), :])
            copies[8].wait()
            part[i, :, pl.ds(half, half)] = project(w[...], x[pl.ds(half, half), :])
        if i == 0:
            pl.semaphore_wait(barrier, YN + n_dp - 1)

        @pl.when(y != i)
        def _():
            y_send(i).start()

    total = part[y]
    for j in range(1, YN):
        p = y_peer(j)
        pltpu.make_async_remote_copy(
            src_ref=part.at[p], dst_ref=recv_y.at[p], send_sem=sy_sem.at[p], recv_sem=ry_sem.at[p],
            device_id={"tensor": p * 2 + zh}, device_id_type=MESH,
        ).wait_recv()
        total += recv_y[p]
    sum_z[...] = total
    zcopy = pltpu.make_async_remote_copy(
        src_ref=sum_z, dst_ref=recv_z, send_sem=sz_sem, recv_sem=rz_sem,
        device_id={"tensor": partner}, device_id_type=MESH,
    )
    zcopy.start()
    zcopy.wait_recv()
    full[y] = total + recv_z[...]
    gathers = []
    for j in range(1, YN):
        p = y_peer(j)
        c = pltpu.make_async_remote_copy(
            src_ref=full.at[y], dst_ref=full.at[y], send_sem=sg_sem.at[j - 1], recv_sem=rg_sem.at[y],
            device_id={"tensor": p * 2 + zh}, device_id_type=MESH,
        )
        c.start()
        gathers.append(c)
    for j in range(1, YN):
        p = y_peer(j)
        pltpu.make_async_remote_copy(
            src_ref=full.at[p], dst_ref=full.at[p], send_sem=sg_sem.at[j - 1], recv_sem=rg_sem.at[p],
            device_id={"tensor": p * 2 + zh}, device_id_type=MESH,
        ).wait_recv()

    copies[9].wait()
    copies[10].wait()
    seg = seg_v[...]
    scale = (EX / TOK) ** 0.5
    masks = [jnp.where(seg == e, scale, 0.0).astype(jnp.float32) for e in range(EX)]
    group = lax.broadcasted_iota(jnp.int32, (EX * KP // 4, 128), 1) // KP
    by_block = []
    for p in range(2):
        low, high = full[2 * p], full[2 * p + 1]
        high_e = jnp.concatenate([high * m for m in masks], axis=0)
        low_e = jnp.concatenate([low * m for m in masks], axis=0)
        low_4 = jnp.concatenate([low] * 4, axis=0)
        g_ref[...] = lax.dot_general(high_e, low_4, NT, precision=HIGH, preferred_element_type=jnp.float32)
        rows = [g_ref[pl.ds(j, EX * KP // 4, stride=4), :] for j in range(4)]
        v_ref[p] = jnp.where(group == 0, rows[0], jnp.where(group == 1, rows[1], jnp.where(group == 2, rows[2], rows[3])))
        by_block.append(lax.dot_general(high, low_e, NT, precision=HIGH, preferred_element_type=jnp.float32))
        ev[p] = v_ref[p, pl.ds(t, EX, stride=8), :]
    ev_out = pltpu.make_async_copy(ev, ev_ref, out_sem.at[0])
    ev_out.start()

    table = jnp.concatenate(
        [jnp.concatenate(by_block, axis=0), (lax.broadcasted_iota(jnp.int32, (BLOCKS, 128), 0) >= KP).astype(jnp.float32)], axis=1
    )
    onehot = (lax.broadcasted_iota(jnp.int32, (BLOCKS, n_dp), 0) == own_v[...]).astype(jnp.float32)
    picked = lax.dot_general(onehot, table, TN, precision=HIGH, preferred_element_type=jnp.float32)
    is_up = picked[:, 128:] > 0.5
    for e in range(EX):
        o_row = jnp.broadcast_to(v_ref[0, pl.ds(t + 8 * e, 1), :], (n_dp, 128))
        up_row = jnp.broadcast_to(v_ref[1, pl.ds(t + 8 * e, 1), :], (n_dp, 128))
        send_d[:, e, :] = jnp.where(is_up, up_row, o_row)
    send_d[:, EX, :] = picked[:, :128]

    def d_copy(dst):
        return pltpu.make_async_remote_copy(
            src_ref=send_d.at[dst, pl.ds(0, EX + 1)], dst_ref=recv_d.at[d, pl.ds(0, EX + 1)],
            send_sem=sd_sem, recv_sem=rd_sem, device_id={"dp": dst}, device_id_type=MESH,
        )

    def d_send(k, carry):
        d_copy(lax.rem(d + k, n_dp)).start()
        return carry

    lax.fori_loop(1, n_dp, d_send, 0)
    recv_d[d] = send_d[d]
    whole = pltpu.make_async_remote_copy(
        src_ref=send_d.at[pl.ds(0, n_dp - 1), pl.ds(0, EX + 1)], dst_ref=recv_d.at[pl.ds(0, n_dp - 1), pl.ds(0, EX + 1)],
        send_sem=sd_sem, recv_sem=rd_sem, device_id={"dp": lax.rem(d + 1, n_dp)}, device_id_type=MESH,
    )
    whole.wait_recv()
    rows_t = recv_d[:, EX, :].T
    fisher = jnp.zeros((KP, 128), jnp.float32)
    for e in range(EX):
        fisher += jnp.dot(
            rows_t[e * KP:(e + 1) * KP], recv_d[:, e, :], precision=HIGH, preferred_element_type=jnp.float32
        )
    f_v[0] = fisher * (1.0 / EXAMPLES)
    f_out = pltpu.make_async_copy(f_v, f_ref, out_sem.at[1])
    f_out.start()

    for i in range(YN):
        @pl.when(y != i)
        def _():
            y_send(i).wait_send()
    zcopy.wait_send()
    for c in gathers:
        c.wait_send()
    whole.wait_send()
    ev_out.wait()
    f_out.wait()


def shards(xo, go, xu, gu, pxo, pgo, pxu, pgu, seg, owner):
    n_dp = lax.axis_size("dp")
    k1, k2 = xo.shape[1], gu.shape[1]
    bf, f32 = jnp.bfloat16, jnp.float32
    hbm = pl.BlockSpec(memory_space=pltpu.HBM)
    dma = pltpu.SemaphoreType.DMA
    return pl.pallas_call(
        functools.partial(kernel, n_dp),
        out_shape=(jax.ShapeDtypeStruct((2, EX, 128), f32), jax.ShapeDtypeStruct((1, KP, 128), f32)),
        in_specs=[hbm] * 10,
        out_specs=(hbm, hbm),
        scratch_shapes=[
            pltpu.VMEM((TOK, k1), bf), pltpu.VMEM((TOK, k1), bf), pltpu.VMEM((TOK, k1), bf), pltpu.VMEM((TOK, k2), bf),
            pltpu.VMEM((KP, k1), bf), pltpu.VMEM((KP, k1), bf), pltpu.VMEM((KP, k1), bf), pltpu.VMEM((KP, k2), bf),
            pltpu.VMEM((1, TOK), jnp.int32), pltpu.VMEM((1, owner.shape[0]), jnp.int32),
            pltpu.VMEM((2, EX, 128), f32), pltpu.VMEM((1, KP, 128), f32),
            pltpu.VMEM((4, KP, TOK), f32), pltpu.VMEM((YN, KP, TOK), f32), pltpu.VMEM((KP, TOK), f32),
            pltpu.VMEM((KP, TOK), f32), pltpu.VMEM((4, KP, TOK), f32), pltpu.VMEM((128, 128), f32), pltpu.VMEM((2, KP, 128), f32),
            pltpu.VMEM((n_dp, 8, 128), f32), pltpu.VMEM((n_dp, 8, 128), f32),
            dma((11,)), dma((2,)), dma((4,)), dma((4,)), dma, dma, dma((3,)), dma((4,)), dma, dma,
        ],
        compiler_params=pltpu.CompilerParams(collective_id=0, has_side_effects=True, vmem_limit_bytes=60 << 20),
    )(xo, go, xu, gu, pxo.T, pgo.T, pxu.T, pgu.T, seg, owner.reshape(1, -1))


def solution(mesh):
    in_specs = (P("dp", "tensor"),) * 4 + (P("tensor", None),) * 4 + (P("dp", None), P())
    out_specs = (P(None, "dp", "tensor"), P("dp", None, "tensor"))
    return jax.shard_map(shards, mesh=mesh, in_specs=in_specs, out_specs=out_specs, check_vma=False)
```

```python
import functools

import jax
import jax.numpy as jnp
from jax import lax
from jax.experimental import pallas as pl
from jax.experimental.pallas import tpu as pltpu
from jax.sharding import PartitionSpec as P

TOK = 256
EX = 4
KP = 32
BLOCKS = 64
EXAMPLES = 256
YN = 4
PLANE = 8
HIGH = lax.Precision.HIGHEST
MESH = pl.DeviceIdType.MESH
NT = (((1,), (1,)), ((), ()))
TN = (((0,), (0,)), ((), ()))


def kernel(
    n_dp,
    xo_ref, go_ref, xu_ref, gu_ref, pxo_ref, pgo_ref, pxu_ref, pgu_ref, seg_ref, own_ref,
    ev_ref, f_ref,
    xo, go, xu, gu, pxo, pgo, pxu, pgu, seg_v, own_v, ev_s, ev_r, f_v,
    part, recv_y, seg_r, sum_z, recv_z, full, g_ref, v_ref, send_d, recv_d,
    in_sem, out_sem, sy_sem, ry_sem, seg_sem, sz_sem, rz_sem, sg_sem, rg_sem, ev_sem, sd_sem, rd_sem,
):
    d = lax.axis_index("dp")
    t = lax.axis_index("tensor")
    y, zh = t // 2, lax.rem(t, 2)
    plane = d // PLANE
    at, core = lax.rem(d, PLANE), lax.rem(d, 2)
    runs = n_dp // PLANE
    ring = 2 * runs
    mid = runs // 2
    z = zh * runs + plane
    held = lax.rem(z + mid, runs) * PLANE + at

    def on_ring(pos):
        pos = lax.rem(pos + ring, ring)
        return pos // runs, lax.rem(pos, runs)

    def ring_peer(step):
        half, line = on_ring(z + step)
        return {"dp": line * PLANE + at, "tensor": y * 2 + half}

    def y_peer(j):
        return lax.rem(y + j, YN)

    def reach(of_core, r):
        low = mid - 1 + of_core
        return lax.rem(r + low, runs) - low

    half = TOK // 2
    loads = [
        (pxo_ref, pxo), (xo_ref, xo), (pgo_ref, pgo), (go_ref, go), (pxu_ref, pxu), (xu_ref, xu), (pgu_ref, pgu),
        (gu_ref.at[pl.ds(0, half)], gu.at[pl.ds(0, half)]), (gu_ref.at[pl.ds(half, half)], gu.at[pl.ds(half, half)]),
        (seg_ref, seg_v), (own_ref, own_v),
    ]
    copies = [pltpu.make_async_copy(s, dst, in_sem.at[i]) for i, (s, dst) in enumerate(loads)]
    for c in copies:
        c.start()

    barrier = pltpu.get_barrier_semaphore()

    def greet(k, carry):
        who = lax.rem(at + k, PLANE)
        half_, line = on_ring(z - reach(lax.rem(who, 2), k // PLANE))
        pl.semaphore_signal(barrier, inc=1, device_id={"dp": line * PLANE + who, "tensor": y * 2 + half_}, device_id_type=MESH)
        return carry

    lax.fori_loop(1, n_dp, greet, 0)
    for step in (mid, -mid):
        pl.semaphore_signal(barrier, inc=1, device_id=ring_peer(step), device_id_type=MESH)
    for j in range(1, YN):
        pl.semaphore_signal(barrier, inc=1, device_id={"tensor": y_peer(j) * 2 + zh}, device_id_type=MESH)

    def project(w, x):
        return lax.dot_general(w, x, NT, preferred_element_type=jnp.float32)

    def y_send(i):
        return pltpu.make_async_remote_copy(
            src_ref=part.at[i], dst_ref=recv_y.at[y], send_sem=sy_sem.at[i], recv_sem=ry_sem.at[y],
            device_id={"tensor": i * 2 + zh}, device_id_type=MESH,
        )

    def y_start(i):
        @pl.when(y != i)
        def _():
            y_send(i).start()

    for i, (w, x) in enumerate(((pxo, xo), (pgo, go), (pxu, xu), (pgu, gu))):
        copies[2 * i].wait()
        copies[2 * i + 1].wait()
        if i < 3:
            part[i] = project(w[...], x[...])
        else:
            part[i, :, pl.ds(0, half)] = project(w[...], x[pl.ds(0, half), :])
            copies[8].wait()
            part[i, :, pl.ds(half, half)] = project(w[...], x[pl.ds(half, half), :])
        if i == 2:
            pl.semaphore_wait(barrier, n_dp - 1 + 2 + YN - 1)
            for k in range(3):
                y_start(k)
    y_start(3)
    copies[9].wait()
    copies[10].wait()
    seg_copy = pltpu.make_async_remote_copy(
        src_ref=seg_v, dst_ref=seg_r, send_sem=seg_sem.at[0], recv_sem=seg_sem.at[1], device_id=ring_peer(mid), device_id_type=MESH,
    )
    seg_copy.start()

    total = part[y]
    for j in range(1, YN):
        p = y_peer(j)
        pltpu.make_async_remote_copy(
            src_ref=part.at[p], dst_ref=recv_y.at[p], send_sem=sy_sem.at[p], recv_sem=ry_sem.at[p],
            device_id={"tensor": p * 2 + zh}, device_id_type=MESH,
        ).wait_recv()
        total += recv_y[p]
    sum_z[...] = total
    swaps = [
        pltpu.make_async_remote_copy(
            src_ref=sum_z, dst_ref=recv_z.at[i], send_sem=sz_sem.at[i], recv_sem=rz_sem.at[i],
            device_id=ring_peer(step), device_id_type=MESH,
        )
        for i, step in enumerate((mid, -mid))
    ]
    for c in swaps:
        c.start()
    for c in swaps:
        c.wait_recv()
    full[y] = recv_z[0] + recv_z[1]
    gathers = []
    for j in range(1, YN):
        p = y_peer(j)
        c = pltpu.make_async_remote_copy(
            src_ref=full.at[y], dst_ref=full.at[y], send_sem=sg_sem.at[j - 1], recv_sem=rg_sem.at[y],
            device_id={"tensor": p * 2 + zh}, device_id_type=MESH,
        )
        c.start()
        gathers.append(c)
    seg_copy.wait_recv()
    seg = seg_r[...]
    scale = (EX / TOK) ** 0.5
    masks = [jnp.where(seg == e, scale, 0.0).astype(jnp.float32) for e in range(EX)]
    onehot = (lax.broadcasted_iota(jnp.int32, (BLOCKS, n_dp), 0) == own_v[...]).astype(jnp.float32)
    for j in range(1, YN):
        p = y_peer(j)
        pltpu.make_async_remote_copy(
            src_ref=full.at[p], dst_ref=full.at[p], send_sem=sg_sem.at[j - 1], recv_sem=rg_sem.at[p],
            device_id={"tensor": p * 2 + zh}, device_id_type=MESH,
        ).wait_recv()

    group = lax.broadcasted_iota(jnp.int32, (EX * KP // 4, 128), 1) // KP
    by_block = []
    for p in range(2):
        low, high = full[2 * p], full[2 * p + 1]
        high_e = jnp.concatenate([high * m for m in masks], axis=0)
        low_e = jnp.concatenate([low * m for m in masks], axis=0)
        low_4 = jnp.concatenate([low] * 4, axis=0)
        g_ref[...] = lax.dot_general(high_e, low_4, NT, precision=HIGH, preferred_element_type=jnp.float32)
        rows = [g_ref[pl.ds(j, EX * KP // 4, stride=4), :] for j in range(4)]
        v_ref[p] = jnp.where(group == 0, rows[0], jnp.where(group == 1, rows[1], jnp.where(group == 2, rows[2], rows[3])))
        by_block.append(lax.dot_general(high, low_e, NT, precision=HIGH, preferred_element_type=jnp.float32))

    table = jnp.concatenate(
        [jnp.concatenate(by_block, axis=0), (lax.broadcasted_iota(jnp.int32, (BLOCKS, 128), 0) >= KP).astype(jnp.float32)], axis=1
    )
    picked = lax.dot_general(onehot, table, TN, precision=HIGH, preferred_element_type=jnp.float32)
    is_up = picked[:, 128:] > 0.5
    low = mid - 1 + core
    line = lax.broadcasted_iota(jnp.int32, (n_dp, 128), 0) // PLANE
    pos = z + lax.rem(line - z + low + ring, runs) - low
    far_half = lax.rem(pos + ring, ring) >= runs
    for e in range(EX):
        r = [[jnp.broadcast_to(v_ref[p, pl.ds(2 * y + h + 8 * e, 1), :], (n_dp, 128)) for h in range(2)] for p in range(2)]
        send_d[:, e, :] = jnp.where(is_up, jnp.where(far_half, r[1][1], r[1][0]), jnp.where(far_half, r[0][1], r[0][0]))
    send_d[:, EX, :] = picked[:, :128]

    def d_send(k, carry):
        who = lax.rem(at + k, PLANE)
        half_, line_ = on_ring(z + reach(core, lax.rem(k // PLANE + mid, runs)))
        dst = line_ * PLANE + who
        pltpu.make_async_remote_copy(
            src_ref=send_d.at[dst, pl.ds(0, EX + 1)], dst_ref=recv_d.at[held, pl.ds(0, EX + 1)],
            send_sem=sd_sem, recv_sem=rd_sem, device_id={"dp": dst, "tensor": y * 2 + half_}, device_id_type=MESH,
        ).start()
        return carry

    lax.fori_loop(0, mid * PLANE, d_send, 0)
    lax.fori_loop(mid * PLANE + 1, n_dp, d_send, 0)
    recv_d[held] = send_d[d]
    owner_half, _ = on_ring(z + mid)
    for p in range(2):
        ev_s[p] = v_ref[p, pl.ds(2 * y + owner_half, EX, stride=8), :]
    ev_copy = pltpu.make_async_remote_copy(
        src_ref=ev_s, dst_ref=ev_r, send_sem=ev_sem.at[0], recv_sem=ev_sem.at[1], device_id=ring_peer(mid), device_id_type=MESH,
    )
    ev_copy.start()
    for i in range(YN):
        @pl.when(y != i)
        def _():
            y_send(i).wait_send()
    seg_copy.wait_send()
    for c in swaps + gathers:
        c.wait_send()
    ev_copy.wait_recv()
    ev_out = pltpu.make_async_copy(ev_r, ev_ref, out_sem.at[0])
    ev_out.start()
    whole = pltpu.make_async_remote_copy(
        src_ref=send_d.at[pl.ds(0, n_dp - 1), pl.ds(0, EX + 1)], dst_ref=recv_d.at[pl.ds(0, n_dp - 1), pl.ds(0, EX + 1)],
        send_sem=sd_sem, recv_sem=rd_sem, device_id=ring_peer(mid), device_id_type=MESH,
    )
    whole.wait_recv()
    rows_t = recv_d[:, EX, :].T
    fisher = jnp.zeros((KP, 128), jnp.float32)
    for e in range(EX):
        fisher += jnp.dot(
            rows_t[e * KP:(e + 1) * KP], recv_d[:, e, :], precision=HIGH, preferred_element_type=jnp.float32
        )
    f_v[0] = fisher * (1.0 / EXAMPLES)
    f_out = pltpu.make_async_copy(f_v, f_ref, out_sem.at[1])
    f_out.start()
    ev_copy.wait_send()
    whole.wait_send()
    ev_out.wait()
    f_out.wait()


def hand_over(ev_ref, f_ref, ev_out, f_out, sem):
    copies = [pltpu.make_async_copy(ev_ref, ev_out, sem.at[0]), pltpu.make_async_copy(f_ref, f_out, sem.at[1])]
    for c in copies:
        c.start()
    for c in copies:
        c.wait()


def shards(xo, go, xu, gu, pxo, pgo, pxu, pgu, seg, owner):
    n_dp = lax.axis_size("dp")
    k1, k2 = xo.shape[1], gu.shape[1]
    bf, f32, i32 = jnp.bfloat16, jnp.float32, jnp.int32
    hbm = pl.BlockSpec(memory_space=pltpu.HBM)
    dma, vm = pltpu.SemaphoreType.DMA, pltpu.VMEM
    outs = (jax.ShapeDtypeStruct((2, EX, 128), f32), jax.ShapeDtypeStruct((1, KP, 128), f32))
    ev, fisher = pl.pallas_call(
        functools.partial(kernel, n_dp),
        out_shape=outs,
        in_specs=[hbm] * 10,
        out_specs=(hbm, hbm),
        scratch_shapes=[
            vm((TOK, k1), bf), vm((TOK, k1), bf), vm((TOK, k1), bf), vm((TOK, k2), bf),
            vm((KP, k1), bf), vm((KP, k1), bf), vm((KP, k1), bf), vm((KP, k2), bf),
            vm((1, TOK), i32), vm((1, owner.shape[0]), i32), vm((2, EX, 128), f32), vm((2, EX, 128), f32), vm((1, KP, 128), f32),
            vm((4, KP, TOK), f32), vm((YN, KP, TOK), f32), vm((1, TOK), i32), vm((KP, TOK), f32), vm((2, KP, TOK), f32),
            vm((4, KP, TOK), f32), vm((128, 128), f32), vm((2, KP, 128), f32), vm((n_dp, 8, 128), f32), vm((n_dp, 8, 128), f32),
            dma((11,)), dma((2,)), dma((4,)), dma((4,)), dma((2,)), dma((2,)), dma((2,)), dma((3,)), dma((4,)), dma((2,)), dma, dma,
        ],
        compiler_params=pltpu.CompilerParams(collective_id=0, has_side_effects=True, vmem_limit_bytes=60 << 20),
    )(xo, go, xu, gu, pxo.T, pgo.T, pxu.T, pgu.T, seg, owner.reshape(1, -1))
    return pl.pallas_call(
        hand_over, out_shape=outs, in_specs=[hbm, hbm], out_specs=(hbm, hbm), scratch_shapes=[dma((2,))],
    )(ev, fisher)


def solution(mesh):
    in_specs = (P("dp", "tensor"),) * 4 + (P("tensor", None),) * 4 + (P("dp", None), P())
    out_specs = (P(None, "dp", "tensor"), P("dp", None, "tensor"))
    return jax.shard_map(shards, mesh=mesh, in_specs=in_specs, out_specs=out_specs, check_vma=False)
```

```python
import functools

import jax
import jax.numpy as jnp
from jax import lax
from jax.experimental import pallas as pl
from jax.experimental.pallas import tpu as pltpu
from jax.sharding import PartitionSpec as P

TOK = 256
EX = 4
KP = 32
BLOCKS = 64
EXAMPLES = 256
YN = 4
PLANE = 8
HIGH = lax.Precision.HIGHEST
MESH = pl.DeviceIdType.MESH
NT = (((1,), (1,)), ((), ()))
TN = (((0,), (0,)), ((), ()))


def kernel(
    n_dp,
    xo_ref, go_ref, xu_ref, gu_ref, pxo_ref, pgo_ref, pxu_ref, pgu_ref, seg_ref, own_ref,
    ev_ref, f_ref,
    xo, go, xu, gu, pxo, pgo, pxu, pgu, seg_v, own_v, ev_s, ev_r,
    part, recv_y, seg_r, sum_z, recv_z, full, g_ref, v_ref, send_d, recv_d,
    in_sem, sy_sem, ry_sem, seg_sem, sz_sem, rz_sem, sg_sem, rg_sem, ev_sem, sd_sem, rd_sem, met_sem, known_sem,
):
    d = lax.axis_index("dp")
    t = lax.axis_index("tensor")
    y, zh = t // 2, lax.rem(t, 2)
    plane = d // PLANE
    at, core = lax.rem(d, PLANE), lax.rem(d, 2)
    runs = n_dp // PLANE
    ring = 2 * runs
    mid = runs // 2
    z = zh * runs + plane
    held = lax.rem(z + mid, runs) * PLANE + at

    def on_ring(pos):
        pos = lax.rem(pos + ring, ring)
        return pos // runs, lax.rem(pos, runs)

    def ring_peer(step):
        half, line = on_ring(z + step)
        return {"dp": line * PLANE + at, "tensor": y * 2 + half}

    def y_peer(j):
        return lax.rem(y + j, YN)

    def reach(of_core, r):
        low = mid - 1 + of_core
        return lax.rem(r + low, runs) - low

    half = TOK // 2
    loads = [
        (pxo_ref, pxo), (xo_ref, xo), (pgo_ref, pgo), (go_ref, go), (pxu_ref, pxu), (xu_ref, xu), (pgu_ref, pgu),
        (gu_ref.at[pl.ds(0, half)], gu.at[pl.ds(0, half)]), (gu_ref.at[pl.ds(half, half)], gu.at[pl.ds(half, half)]),
        (seg_ref, seg_v), (own_ref, own_v),
    ]
    copies = [pltpu.make_async_copy(s, dst, in_sem.at[i]) for i, (s, dst) in enumerate(loads)]
    for c in copies:
        c.start()

    barrier = pltpu.get_barrier_semaphore()
    near = (2, -2, 1, -1)
    for k in (4, 5, 3, 2, 6, 7, 1):
        pl.semaphore_signal(barrier, inc=1, device_id={"dp": plane * PLANE + lax.rem(at + k, PLANE)}, device_id_type=MESH)
    for step in near:
        pl.semaphore_signal(barrier, inc=1, device_id=ring_peer(step), device_id_type=MESH)
    for j in (2, 1, 3):
        pl.semaphore_signal(barrier, inc=1, device_id={"tensor": y_peer(j) * 2 + zh}, device_id_type=MESH)

    def project(w, x):
        return lax.dot_general(w, x, NT, preferred_element_type=jnp.float32)

    def y_send(i):
        return pltpu.make_async_remote_copy(
            src_ref=part.at[i], dst_ref=recv_y.at[y], send_sem=sy_sem.at[i], recv_sem=ry_sem.at[y],
            device_id={"tensor": i * 2 + zh}, device_id_type=MESH,
        )

    def y_start(i):
        @pl.when(y != i)
        def _():
            y_send(i).start()

    for i, (w, x) in enumerate(((pxo, xo), (pgo, go), (pxu, xu), (pgu, gu))):
        copies[2 * i].wait()
        copies[2 * i + 1].wait()
        if i < 3:
            part[i] = project(w[...], x[...])
        else:
            part[i, :, pl.ds(0, half)] = project(w[...], x[pl.ds(0, half), :])
            copies[8].wait()
            part[i, :, pl.ds(half, half)] = project(w[...], x[pl.ds(half, half), :])
        if i == 2:
            pl.semaphore_wait(barrier, PLANE - 1 + len(near) + YN - 1)
            for k in range(3):
                y_start(k)
    y_start(3)
    for step in near:
        pl.semaphore_signal(met_sem, inc=1, device_id=ring_peer(step), device_id_type=MESH)
    copies[9].wait()
    copies[10].wait()
    total = part[y]
    for j in range(1, YN):
        p = y_peer(j)
        pltpu.make_async_remote_copy(
            src_ref=part.at[p], dst_ref=recv_y.at[p], send_sem=sy_sem.at[p], recv_sem=ry_sem.at[p],
            device_id={"tensor": p * 2 + zh}, device_id_type=MESH,
        ).wait_recv()
        total += recv_y[p]
    sum_z[...] = total
    pl.semaphore_wait(met_sem, len(near))
    swaps = [
        pltpu.make_async_remote_copy(
            src_ref=sum_z, dst_ref=recv_z.at[i], send_sem=sz_sem.at[i], recv_sem=rz_sem.at[i],
            device_id=ring_peer(step), device_id_type=MESH,
        )
        for i, step in enumerate((mid, -mid))
    ]
    for c in swaps:
        c.start()
    for step in near[:2]:
        pl.semaphore_signal(known_sem, inc=1, device_id=ring_peer(step), device_id_type=MESH)
    seg_copy = pltpu.make_async_remote_copy(
        src_ref=seg_v, dst_ref=seg_r, send_sem=seg_sem.at[0], recv_sem=seg_sem.at[1], device_id=ring_peer(mid), device_id_type=MESH,
    )
    seg_copy.start()
    for c in swaps:
        c.wait_recv()
    full[y] = recv_z[0] + recv_z[1]
    gathers = []
    for j in range(1, YN):
        p = y_peer(j)
        c = pltpu.make_async_remote_copy(
            src_ref=full.at[y], dst_ref=full.at[y], send_sem=sg_sem.at[j - 1], recv_sem=rg_sem.at[y],
            device_id={"tensor": p * 2 + zh}, device_id_type=MESH,
        )
        c.start()
        gathers.append(c)
    seg_copy.wait_recv()
    seg = seg_r[...]
    scale = (EX / TOK) ** 0.5
    masks = [jnp.where(seg == e, scale, 0.0).astype(jnp.float32) for e in range(EX)]
    onehot = (lax.broadcasted_iota(jnp.int32, (BLOCKS, n_dp), 0) == own_v[...]).astype(jnp.float32)
    for j in range(1, YN):
        p = y_peer(j)
        pltpu.make_async_remote_copy(
            src_ref=full.at[p], dst_ref=full.at[p], send_sem=sg_sem.at[j - 1], recv_sem=rg_sem.at[p],
            device_id={"tensor": p * 2 + zh}, device_id_type=MESH,
        ).wait_recv()

    group = lax.broadcasted_iota(jnp.int32, (EX * KP // 4, 128), 1) // KP
    by_block = []
    for p in range(2):
        low, high = full[2 * p], full[2 * p + 1]
        high_e = jnp.concatenate([high * m for m in masks], axis=0)
        low_e = jnp.concatenate([low * m for m in masks], axis=0)
        low_4 = jnp.concatenate([low] * 4, axis=0)
        g_ref[...] = lax.dot_general(high_e, low_4, NT, precision=HIGH, preferred_element_type=jnp.float32)
        rows = [g_ref[pl.ds(j, EX * KP // 4, stride=4), :] for j in range(4)]
        v_ref[p] = jnp.where(group == 0, rows[0], jnp.where(group == 1, rows[1], jnp.where(group == 2, rows[2], rows[3])))
        by_block.append(lax.dot_general(high, low_e, NT, precision=HIGH, preferred_element_type=jnp.float32))

    table = jnp.concatenate(
        [jnp.concatenate(by_block, axis=0), (lax.broadcasted_iota(jnp.int32, (BLOCKS, 128), 0) >= KP).astype(jnp.float32)], axis=1
    )
    picked = lax.dot_general(onehot, table, TN, precision=HIGH, preferred_element_type=jnp.float32)
    is_up = picked[:, 128:] > 0.5
    low = mid - 1 + core
    line = lax.broadcasted_iota(jnp.int32, (n_dp, 128), 0) // PLANE
    pos = z + lax.rem(line - z + low + ring, runs) - low
    far_half = lax.rem(pos + ring, ring) >= runs
    for e in range(EX):
        r = [[jnp.broadcast_to(v_ref[p, pl.ds(2 * y + h + 8 * e, 1), :], (n_dp, 128)) for h in range(2)] for p in range(2)]
        send_d[:, e, :] = jnp.where(is_up, jnp.where(far_half, r[1][1], r[1][0]), jnp.where(far_half, r[0][1], r[0][0]))
    send_d[:, EX, :] = picked[:, :128]

    def d_send(k):
        who = lax.rem(at + k % PLANE, PLANE)
        half_, line_ = on_ring(z + reach(core, k // PLANE))
        dst = line_ * PLANE + who
        pltpu.make_async_remote_copy(
            src_ref=send_d.at[dst, pl.ds(0, EX + 1)], dst_ref=recv_d.at[held, pl.ds(0, EX + 1)],
            send_sem=sd_sem, recv_sem=rd_sem, device_id={"dp": dst, "tensor": y * 2 + half_}, device_id_type=MESH,
        ).start()

    pl.semaphore_wait(known_sem, 2)

    def hops(k):
        return min(k // PLANE, runs - k // PLANE) + min(k % PLANE, PLANE - k % PLANE) // 2

    for k in sorted(range(1, n_dp), key=hops, reverse=True):
        d_send(k)
    recv_d[held] = send_d[d]
    owner_half, _ = on_ring(z + mid)
    for p in range(2):
        ev_s[p] = v_ref[p, pl.ds(2 * y + owner_half, EX, stride=8), :]
    ev_copy = pltpu.make_async_remote_copy(
        src_ref=ev_s, dst_ref=ev_r, send_sem=ev_sem.at[0], recv_sem=ev_sem.at[1], device_id=ring_peer(mid), device_id_type=MESH,
    )
    ev_copy.start()
    for i in range(YN):
        @pl.when(y != i)
        def _():
            y_send(i).wait_send()
    seg_copy.wait_send()
    for c in swaps + gathers:
        c.wait_send()
    whole = pltpu.make_async_remote_copy(
        src_ref=send_d.at[pl.ds(0, n_dp - 1), pl.ds(0, EX + 1)], dst_ref=recv_d.at[pl.ds(0, n_dp - 1), pl.ds(0, EX + 1)],
        send_sem=sd_sem, recv_sem=rd_sem, device_id=ring_peer(mid), device_id_type=MESH,
    )
    whole.wait_recv()
    rows_t = recv_d[:, EX, :].T
    fisher = jnp.zeros((KP, 128), jnp.float32)
    for e in range(EX):
        fisher += jnp.dot(
            rows_t[e * KP:(e + 1) * KP], recv_d[:, e, :], precision=HIGH, preferred_element_type=jnp.float32
        )
    f_ref[0] = fisher * (1.0 / EXAMPLES)
    ev_copy.wait()
    ev_ref[...] = ev_r[...]
    whole.wait_send()


def hand_over(ev_ref, f_ref, ev_out, f_out, sem):
    copies = [pltpu.make_async_copy(ev_ref, ev_out, sem.at[0]), pltpu.make_async_copy(f_ref, f_out, sem.at[1])]
    for c in copies:
        c.start()
    for c in copies:
        c.wait()


def shards(xo, go, xu, gu, pxo, pgo, pxu, pgu, seg, owner):
    n_dp = lax.axis_size("dp")
    k1, k2 = xo.shape[1], gu.shape[1]
    bf, f32, i32 = jnp.bfloat16, jnp.float32, jnp.int32
    hbm, vmem = pl.BlockSpec(memory_space=pltpu.HBM), pl.BlockSpec(memory_space=pltpu.VMEM)
    dma, vm = pltpu.SemaphoreType.DMA, pltpu.VMEM
    outs = (jax.ShapeDtypeStruct((2, EX, 128), f32), jax.ShapeDtypeStruct((1, KP, 128), f32))
    args = (xo, go, xu, gu, pxo.T, pgo.T, pxu.T, pgu.T, seg, owner.reshape(1, -1))
    ev, fisher = pl.pallas_call(
        functools.partial(kernel, n_dp),
        out_shape=outs,
        in_specs=[hbm] * 10,
        out_specs=(vmem, vmem),
        scratch_shapes=[
            vm((TOK, k1), bf), vm((TOK, k1), bf), vm((TOK, k1), bf), vm((TOK, k2), bf),
            vm((KP, k1), bf), vm((KP, k1), bf), vm((KP, k1), bf), vm((KP, k2), bf),
            vm((1, TOK), i32), vm((1, owner.shape[0]), i32), vm((2, EX, 128), f32), vm((2, EX, 128), f32),
            vm((4, KP, TOK), f32), vm((YN, KP, TOK), f32), vm((1, TOK), i32), vm((KP, TOK), f32), vm((2, KP, TOK), f32),
            vm((4, KP, TOK), f32), vm((128, 128), f32), vm((2, KP, 128), f32), vm((n_dp, 8, 128), f32), vm((n_dp, 8, 128), f32),
            dma((11,)), dma((4,)), dma((4,)), dma((2,)), dma((2,)), dma((2,)), dma((3,)), dma((4,)), dma((2,)), dma, dma,
            pltpu.SemaphoreType.REGULAR, pltpu.SemaphoreType.REGULAR,
        ],
        compiler_params=pltpu.CompilerParams(collective_id=0, has_side_effects=True, vmem_limit_bytes=32 << 20),
    )(*(pltpu.with_memory_space_constraint(a, pltpu.HBM) for a in args))
    return pl.pallas_call(
        hand_over, out_shape=outs, in_specs=[vmem, vmem], out_specs=(hbm, hbm), scratch_shapes=[dma((2,))],
        compiler_params=pltpu.CompilerParams(vmem_limit_bytes=4 << 20),
    )(ev, fisher)


def solution(mesh):
    in_specs = (P("dp", "tensor"),) * 4 + (P("tensor", None),) * 4 + (P("dp", None), P())
    out_specs = (P(None, "dp", "tensor"), P("dp", None, "tensor"))
    return jax.shard_map(shards, mesh=mesh, in_specs=in_specs, out_specs=out_specs, check_vma=False)
```

```python
import functools

import jax
import jax.numpy as jnp
from jax import lax
from jax.experimental import pallas as pl
from jax.experimental.pallas import tpu as pltpu
from jax.sharding import PartitionSpec as P

TOK = 256
EX = 4
KP = 32
BLOCKS = 64
EXAMPLES = 256
YN = 4
PLANE = 8
HIGH = lax.Precision.HIGHEST
MESH = pl.DeviceIdType.MESH
NT = (((1,), (1,)), ((), ()))
TN = (((0,), (0,)), ((), ()))


def split(x):
    top = x.astype(jnp.bfloat16)
    return top, (x - top.astype(jnp.float32)).astype(jnp.bfloat16)


def dot3(a, b, dims):
    (a1, a2), (b1, b2) = split(a), split(b)

    def one(p, q):
        return lax.dot_general(p, q, dims, preferred_element_type=jnp.float32)

    return one(a1, b1) + (one(a1, b2) + one(a2, b1))


def kernel(
    n_dp,
    xo_ref, go_ref, xu_ref, gu_ref, pxo_ref, pgo_ref, pxu_ref, pgu_ref, seg_ref, own_ref,
    ev_ref, f_ref,
    xo, go, xu, gu, pxo, pgo, pxu, pgu, seg_v, own_v, ev_s, ev_r,
    part, recv_y, seg_r, sum_z, recv_z, full, g_ref, v_ref, send_d, recv_d,
    in_sem, sy_sem, ry_sem, seg_sem, sz_sem, rz_sem, sg_sem, rg_sem, ev_sem, sd_sem, rd_sem, met_sem, known_sem,
):
    d = lax.axis_index("dp")
    t = lax.axis_index("tensor")
    y, zh = t // 2, lax.rem(t, 2)
    plane = d // PLANE
    at, core = lax.rem(d, PLANE), lax.rem(d, 2)
    runs = n_dp // PLANE
    ring = 2 * runs
    mid = runs // 2
    z = zh * runs + plane
    held = lax.rem(z + mid, runs) * PLANE + at

    def on_ring(pos):
        pos = lax.rem(pos + ring, ring)
        return pos // runs, lax.rem(pos, runs)

    def ring_peer(step):
        half, line = on_ring(z + step)
        return {"dp": line * PLANE + at, "tensor": y * 2 + half}

    def y_peer(j):
        return lax.rem(y + j, YN)

    def reach(of_core, r):
        low = mid - 1 + of_core
        return lax.rem(r + low, runs) - low

    half = TOK // 2
    loads = [
        (pxo_ref, pxo), (xo_ref, xo), (pgo_ref, pgo), (go_ref, go), (pxu_ref, pxu), (xu_ref, xu), (pgu_ref, pgu),
        (gu_ref.at[pl.ds(0, half)], gu.at[pl.ds(0, half)]), (gu_ref.at[pl.ds(half, half)], gu.at[pl.ds(half, half)]),
        (seg_ref, seg_v), (own_ref, own_v),
    ]
    copies = [pltpu.make_async_copy(s, dst, in_sem.at[i]) for i, (s, dst) in enumerate(loads)]
    for c in copies:
        c.start()

    barrier = pltpu.get_barrier_semaphore()
    near = (2, -2, 1, -1)
    for k in (4, 5, 3, 2, 6, 7, 1):
        pl.semaphore_signal(barrier, inc=1, device_id={"dp": plane * PLANE + lax.rem(at + k, PLANE)}, device_id_type=MESH)
    for step in near:
        pl.semaphore_signal(barrier, inc=1, device_id=ring_peer(step), device_id_type=MESH)
    for j in (2, 1, 3):
        pl.semaphore_signal(barrier, inc=1, device_id={"tensor": y_peer(j) * 2 + zh}, device_id_type=MESH)

    def project(w, x):
        return lax.dot_general(w, x, NT, preferred_element_type=jnp.float32)

    def y_send(i):
        return pltpu.make_async_remote_copy(
            src_ref=part.at[i], dst_ref=recv_y.at[y], send_sem=sy_sem.at[i], recv_sem=ry_sem.at[y],
            device_id={"tensor": i * 2 + zh}, device_id_type=MESH,
        )

    def y_start(i):
        @pl.when(y != i)
        def _():
            y_send(i).start()

    for i, (w, x) in enumerate(((pxo, xo), (pgo, go), (pxu, xu), (pgu, gu))):
        copies[2 * i].wait()
        copies[2 * i + 1].wait()
        if i < 3:
            part[i] = project(w[...], x[...])
        else:
            part[i, :, pl.ds(0, half)] = project(w[...], x[pl.ds(0, half), :])
            copies[8].wait()
            part[i, :, pl.ds(half, half)] = project(w[...], x[pl.ds(half, half), :])
        if i == 2:
            pl.semaphore_wait(barrier, PLANE - 1 + len(near) + YN - 1)
            for k in range(3):
                y_start(k)
    y_start(3)
    for step in near:
        pl.semaphore_signal(met_sem, inc=1, device_id=ring_peer(step), device_id_type=MESH)
    copies[9].wait()
    copies[10].wait()
    total = part[y]
    for j in range(1, YN):
        p = y_peer(j)
        pltpu.make_async_remote_copy(
            src_ref=part.at[p], dst_ref=recv_y.at[p], send_sem=sy_sem.at[p], recv_sem=ry_sem.at[p],
            device_id={"tensor": p * 2 + zh}, device_id_type=MESH,
        ).wait_recv()
        total += recv_y[p]
    sum_z[...] = total
    pl.semaphore_wait(met_sem, len(near))
    swaps = [
        pltpu.make_async_remote_copy(
            src_ref=sum_z, dst_ref=recv_z.at[i], send_sem=sz_sem.at[i], recv_sem=rz_sem.at[i],
            device_id=ring_peer(step), device_id_type=MESH,
        )
        for i, step in enumerate((mid, -mid))
    ]
    for c in swaps:
        c.start()
    for step in near[:2]:
        pl.semaphore_signal(known_sem, inc=1, device_id=ring_peer(step), device_id_type=MESH)
    seg_copy = pltpu.make_async_remote_copy(
        src_ref=seg_v, dst_ref=seg_r, send_sem=seg_sem.at[0], recv_sem=seg_sem.at[1], device_id=ring_peer(mid), device_id_type=MESH,
    )
    seg_copy.start()
    for c in swaps:
        c.wait_recv()
    full[y] = recv_z[0] + recv_z[1]
    gathers = []
    for j in range(1, YN):
        p = y_peer(j)
        c = pltpu.make_async_remote_copy(
            src_ref=full.at[y], dst_ref=full.at[y], send_sem=sg_sem.at[j - 1], recv_sem=rg_sem.at[y],
            device_id={"tensor": p * 2 + zh}, device_id_type=MESH,
        )
        c.start()
        gathers.append(c)
    seg_copy.wait_recv()
    seg = seg_r[...]
    scale = (EX / TOK) ** 0.5
    masks = [jnp.where(seg == e, scale, 0.0).astype(jnp.float32) for e in range(EX)]
    onehot = (lax.broadcasted_iota(jnp.int32, (BLOCKS, n_dp), 0) == own_v[...]).astype(jnp.bfloat16)
    for j in range(1, YN):
        p = y_peer(j)
        pltpu.make_async_remote_copy(
            src_ref=full.at[p], dst_ref=full.at[p], send_sem=sg_sem.at[j - 1], recv_sem=rg_sem.at[p],
            device_id={"tensor": p * 2 + zh}, device_id_type=MESH,
        ).wait_recv()

    group = lax.broadcasted_iota(jnp.int32, (EX * KP // 4, 128), 1) // KP
    by_block = []
    for p in range(2):
        low, high = full[2 * p], full[2 * p + 1]
        high_e = jnp.concatenate([high * m for m in masks], axis=0)
        low_e = jnp.concatenate([low * m for m in masks], axis=0)
        low_4 = jnp.concatenate([low] * 4, axis=0)
        g_ref[...] = dot3(high_e, low_4, NT)
        rows = [g_ref[pl.ds(j, EX * KP // 4, stride=4), :] for j in range(4)]
        v_ref[p] = jnp.where(group == 0, rows[0], jnp.where(group == 1, rows[1], jnp.where(group == 2, rows[2], rows[3])))
        by_block.append(dot3(high, low_e, NT))

    table = jnp.concatenate(
        [jnp.concatenate(by_block, axis=0), (lax.broadcasted_iota(jnp.int32, (BLOCKS, 128), 0) >= KP).astype(jnp.float32)], axis=1
    )
    picked = sum(lax.dot_general(onehot, part_, TN, preferred_element_type=jnp.float32) for part_ in split(table))
    is_up = picked[:, 128:] > 0.5
    low = mid - 1 + core
    line = lax.broadcasted_iota(jnp.int32, (n_dp, 128), 0) // PLANE
    pos = z + lax.rem(line - z + low + ring, runs) - low
    far_half = lax.rem(pos + ring, ring) >= runs
    for e in range(EX):
        r = [[jnp.broadcast_to(v_ref[p, pl.ds(2 * y + h + 8 * e, 1), :], (n_dp, 128)) for h in range(2)] for p in range(2)]
        send_d[:, e, :] = jnp.where(is_up, jnp.where(far_half, r[1][1], r[1][0]), jnp.where(far_half, r[0][1], r[0][0]))
    send_d[:, EX, :] = picked[:, :128]

    def d_send(k):
        who = lax.rem(at + k % PLANE, PLANE)
        half_, line_ = on_ring(z + reach(core, k // PLANE))
        dst = line_ * PLANE + who
        pltpu.make_async_remote_copy(
            src_ref=send_d.at[dst, pl.ds(0, EX + 1)], dst_ref=recv_d.at[held, pl.ds(0, EX + 1)],
            send_sem=sd_sem, recv_sem=rd_sem, device_id={"dp": dst, "tensor": y * 2 + half_}, device_id_type=MESH,
        ).start()

    pl.semaphore_wait(known_sem, 2)

    def hops(k):
        return min(k // PLANE, runs - k // PLANE) + min(k % PLANE, PLANE - k % PLANE) // 2

    owner_half, _ = on_ring(z + mid)
    for p in range(2):
        ev_s[p] = v_ref[p, pl.ds(2 * y + owner_half, EX, stride=8), :]
    ev_copy = pltpu.make_async_remote_copy(
        src_ref=ev_s, dst_ref=ev_r, send_sem=ev_sem.at[0], recv_sem=ev_sem.at[1], device_id=ring_peer(mid), device_id_type=MESH,
    )
    ev_copy.start()

    for k in sorted(range(1, n_dp), key=hops, reverse=True):
        d_send(k)
    recv_d[held] = send_d[d]
    for i in range(YN):
        @pl.when(y != i)
        def _():
            y_send(i).wait_send()
    seg_copy.wait_send()
    for c in swaps + gathers:
        c.wait_send()
    whole = pltpu.make_async_remote_copy(
        src_ref=send_d.at[pl.ds(0, n_dp - 1), pl.ds(0, EX + 1)], dst_ref=recv_d.at[pl.ds(0, n_dp - 1), pl.ds(0, EX + 1)],
        send_sem=sd_sem, recv_sem=rd_sem, device_id=ring_peer(mid), device_id_type=MESH,
    )
    whole.wait_recv()
    rows_t = recv_d[:, EX, :].T
    fisher = jnp.zeros((KP, 128), jnp.float32)
    for e in range(EX):
        fisher += dot3(rows_t[e * KP:(e + 1) * KP], recv_d[:, e, :], (((1,), (0,)), ((), ())))
    f_ref[0] = fisher * (1.0 / EXAMPLES)
    ev_copy.wait()
    ev_ref[...] = ev_r[...]
    whole.wait_send()


def hand_over(ev_ref, f_ref, ev_out, f_out, sem):
    copies = [pltpu.make_async_copy(ev_ref, ev_out, sem.at[0]), pltpu.make_async_copy(f_ref, f_out, sem.at[1])]
    for c in copies:
        c.start()
    for c in copies:
        c.wait()


def shards(xo, go, xu, gu, pxo, pgo, pxu, pgu, seg, owner):
    n_dp = lax.axis_size("dp")
    k1, k2 = xo.shape[1], gu.shape[1]
    bf, f32, i32 = jnp.bfloat16, jnp.float32, jnp.int32
    hbm, vmem = pl.BlockSpec(memory_space=pltpu.HBM), pl.BlockSpec(memory_space=pltpu.VMEM)
    dma, vm = pltpu.SemaphoreType.DMA, pltpu.VMEM
    outs = (jax.ShapeDtypeStruct((2, EX, 128), f32), jax.ShapeDtypeStruct((1, KP, 128), f32))
    args = (xo, go, xu, gu, pxo.T, pgo.T, pxu.T, pgu.T, seg, owner.reshape(1, -1))
    ev, fisher = pl.pallas_call(
        functools.partial(kernel, n_dp),
        out_shape=outs,
        in_specs=[hbm] * 10,
        out_specs=(vmem, vmem),
        scratch_shapes=[
            vm((TOK, k1), bf), vm((TOK, k1), bf), vm((TOK, k1), bf), vm((TOK, k2), bf),
            vm((KP, k1), bf), vm((KP, k1), bf), vm((KP, k1), bf), vm((KP, k2), bf),
            vm((1, TOK), i32), vm((1, owner.shape[0]), i32), vm((2, EX, 128), f32), vm((2, EX, 128), f32),
            vm((4, KP, TOK), f32), vm((YN, KP, TOK), f32), vm((1, TOK), i32), vm((KP, TOK), f32), vm((2, KP, TOK), f32),
            vm((4, KP, TOK), f32), vm((128, 128), f32), vm((2, KP, 128), f32), vm((n_dp, 8, 128), f32), vm((n_dp, 8, 128), f32),
            dma((11,)), dma((4,)), dma((4,)), dma((2,)), dma((2,)), dma((2,)), dma((3,)), dma((4,)), dma((2,)), dma, dma,
            pltpu.SemaphoreType.REGULAR, pltpu.SemaphoreType.REGULAR,
        ],
        compiler_params=pltpu.CompilerParams(collective_id=0, has_side_effects=True, vmem_limit_bytes=32 << 20),
    )(*(pltpu.with_memory_space_constraint(a, pltpu.HBM) for a in args))
    return pl.pallas_call(
        hand_over, out_shape=outs, in_specs=[vmem, vmem], out_specs=(hbm, hbm), scratch_shapes=[dma((2,))],
        compiler_params=pltpu.CompilerParams(vmem_limit_bytes=4 << 20),
    )(ev, fisher)


def solution(mesh):
    in_specs = (P("dp", "tensor"),) * 4 + (P("tensor", None),) * 4 + (P("dp", None), P())
    out_specs = (P(None, "dp", "tensor"), P("dp", None, "tensor"))
    return jax.shard_map(shards, mesh=mesh, in_specs=in_specs, out_specs=out_specs, check_vma=False)
```

```python
import functools

import jax
import jax.numpy as jnp
from jax import lax
from jax.experimental import pallas as pl
from jax.experimental.pallas import tpu as pltpu
from jax.sharding import PartitionSpec as P

TOK = 256
EX = 4
KP = 32
BLOCKS = 64
EXAMPLES = 256
YN = 4
PLANE = 8
MESH = pl.DeviceIdType.MESH
NT = (((1,), (1,)), ((), ()))
TN = (((0,), (0,)), ((), ()))


def split(x):
    top = x.astype(jnp.bfloat16)
    return top, (x - top.astype(jnp.float32)).astype(jnp.bfloat16)


def dot3(a, b, dims):
    (a1, a2), (b1, b2) = a, b

    def one(p, q):
        return lax.dot_general(p, q, dims, preferred_element_type=jnp.float32)

    return one(a1, b1) + (one(a1, b2) + one(a2, b1))


def kernel(
    n_dp,
    xo_ref, go_ref, xu_ref, gu_ref, pxo_ref, pgo_ref, pxu_ref, pgu_ref, seg_ref, own_ref,
    ev_ref, f_ref,
    xo, go, xu, gu, pxo, pgo, pxu, pgu, seg_v, own_v, ev_s, ev_r,
    part, recv_y, seg_r, sum_z, recv_z, full, g_ref, v_ref, send_d, recv_d,
    in_sem, sy_sem, ry_sem, seg_sem, sz_sem, rz_sem, sg_sem, rg_sem, ev_sem, sd_sem, rd_sem, met_sem, known_sem,
):
    d = lax.axis_index("dp")
    t = lax.axis_index("tensor")
    y, zh = t // 2, lax.rem(t, 2)
    plane = d // PLANE
    at, core = lax.rem(d, PLANE), lax.rem(d, 2)
    runs = n_dp // PLANE
    ring = 2 * runs
    mid = runs // 2
    z = zh * runs + plane
    held = lax.rem(z + mid, runs) * PLANE + at

    def on_ring(pos):
        pos = lax.rem(pos + ring, ring)
        return pos // runs, lax.rem(pos, runs)

    def ring_peer(step):
        half, line = on_ring(z + step)
        return {"dp": line * PLANE + at, "tensor": y * 2 + half}

    def y_peer(j):
        return lax.rem(y + j, YN)

    def reach(of_core, r):
        low = mid - 1 + of_core
        return lax.rem(r + low, runs) - low

    half = TOK // 2
    loads = [
        (pxo_ref, pxo), (xo_ref, xo), (pgo_ref, pgo), (go_ref, go), (pxu_ref, pxu), (xu_ref, xu), (pgu_ref, pgu),
        (gu_ref.at[pl.ds(0, half)], gu.at[pl.ds(0, half)]), (gu_ref.at[pl.ds(half, half)], gu.at[pl.ds(half, half)]),
        (seg_ref, seg_v), (own_ref, own_v),
    ]
    copies = [pltpu.make_async_copy(s, dst, in_sem.at[i]) for i, (s, dst) in enumerate(loads)]
    for c in copies:
        c.start()

    barrier = pltpu.get_barrier_semaphore()
    near = (2, -2, 1, -1)
    for k in (4, 5, 3, 2, 6, 7, 1):
        pl.semaphore_signal(barrier, inc=1, device_id={"dp": plane * PLANE + lax.rem(at + k, PLANE)}, device_id_type=MESH)
    for step in near:
        pl.semaphore_signal(barrier, inc=1, device_id=ring_peer(step), device_id_type=MESH)
    for j in (2, 1, 3):
        pl.semaphore_signal(barrier, inc=1, device_id={"tensor": y_peer(j) * 2 + zh}, device_id_type=MESH)

    def project(w, x):
        return lax.dot_general(w, x, NT, preferred_element_type=jnp.float32)

    def y_send(i, h):
        return pltpu.make_async_remote_copy(
            src_ref=part.at[i, h], dst_ref=recv_y.at[y, h], send_sem=sy_sem.at[i, h], recv_sem=ry_sem.at[y, h],
            device_id={"tensor": i * 2 + zh}, device_id_type=MESH,
        )

    def y_start(i, h):
        @pl.when(y != i)
        def _():
            y_send(i, h).start()

    for i, (w, x) in enumerate(((pxo, xo), (pgo, go), (pxu, xu))):
        copies[2 * i].wait()
        copies[2 * i + 1].wait()
        q = project(w[...], x[...])
        part[i, 0] = q[:, :half]
        part[i, 1] = q[:, half:]
    pl.semaphore_wait(barrier, PLANE - 1 + len(near) + YN - 1)
    for h in range(2):
        for i in range(3):
            y_start(i, h)
    copies[6].wait()
    for h in range(2):
        copies[7 + h].wait()
        part[3, h] = project(pgu[...], gu[pl.ds(h * half, half), :])
        y_start(3, h)
    for step in near:
        pl.semaphore_signal(met_sem, inc=1, device_id=ring_peer(step), device_id_type=MESH)
    copies[9].wait()
    copies[10].wait()

    swaps = []
    for h in range(2):
        total = part[y, h]
        for j in range(1, YN):
            p = y_peer(j)
            pltpu.make_async_remote_copy(
                src_ref=part.at[p, h], dst_ref=recv_y.at[p, h], send_sem=sy_sem.at[p, h], recv_sem=ry_sem.at[p, h],
                device_id={"tensor": p * 2 + zh}, device_id_type=MESH,
            ).wait_recv()
            total += recv_y[p, h]
        sum_z[h] = total
        if h == 0:
            pl.semaphore_wait(met_sem, len(near))
        swaps.append([
            pltpu.make_async_remote_copy(
                src_ref=sum_z.at[h], dst_ref=recv_z.at[i, h], send_sem=sz_sem.at[i, h], recv_sem=rz_sem.at[i, h],
                device_id=ring_peer(step), device_id_type=MESH,
            )
            for i, step in enumerate((mid, -mid))
        ])
        for c in swaps[h]:
            c.start()
    for step in near[:2]:
        pl.semaphore_signal(known_sem, inc=1, device_id=ring_peer(step), device_id_type=MESH)
    seg_copy = pltpu.make_async_remote_copy(
        src_ref=seg_v, dst_ref=seg_r, send_sem=seg_sem.at[0], recv_sem=seg_sem.at[1], device_id=ring_peer(mid), device_id_type=MESH,
    )
    seg_copy.start()
    gathers = []
    for h in range(2):
        for c in swaps[h]:
            c.wait_recv()
        full[y, h] = recv_z[0, h] + recv_z[1, h]
        for j in (2, 1, 3):
            p = y_peer(j)
            c = pltpu.make_async_remote_copy(
                src_ref=full.at[y, h], dst_ref=full.at[y, h], send_sem=sg_sem.at[j - 1, h], recv_sem=rg_sem.at[y, h],
                device_id={"tensor": p * 2 + zh}, device_id_type=MESH,
            )
            c.start()
            gathers.append(c)
    seg_copy.wait_recv()
    seg = seg_r[...]
    scale = (EX / TOK) ** 0.5
    masks = [jnp.where(seg == e, scale, 0.0).astype(jnp.bfloat16) for e in range(EX)]
    onehot = (lax.broadcasted_iota(jnp.int32, (BLOCKS, n_dp), 0) == own_v[...]).astype(jnp.bfloat16)
    block_is_up = (lax.broadcasted_iota(jnp.int32, (BLOCKS, 128), 0) >= KP).astype(jnp.bfloat16)
    is_up = lax.dot_general(onehot, block_is_up, TN, preferred_element_type=jnp.float32) > 0.5
    low = mid - 1 + core
    line = lax.broadcasted_iota(jnp.int32, (n_dp, 128), 0) // PLANE
    pos = z + lax.rem(line - z + low + ring, runs) - low
    far_half = lax.rem(pos + ring, ring) >= runs
    group = lax.broadcasted_iota(jnp.int32, (EX * KP // 4, 128), 1) // KP

    def by_group(rows):
        return jnp.where(group == 0, rows[0], jnp.where(group == 1, rows[1], jnp.where(group == 2, rows[2], rows[3])))

    outer = [0.0, 0.0]
    for h in range(2):
        for j in range(1, YN):
            p = y_peer(j)
            pltpu.make_async_remote_copy(
                src_ref=full.at[p, h], dst_ref=full.at[p, h], send_sem=sg_sem.at[j - 1, h], recv_sem=rg_sem.at[p, h],
                device_id={"tensor": p * 2 + zh}, device_id_type=MESH,
            ).wait_recv()
        m_h = [m[:, h * half:(h + 1) * half] for m in masks]
        for p in range(2):
            low, high = split(full[2 * p, h]), split(full[2 * p + 1, h])
            low_4 = [jnp.concatenate([v] * 4, axis=0) for v in low]
            high_e = [jnp.concatenate([v * m for m in m_h], axis=0) for v in high]
            outer[p] += dot3(high_e, low_4, NT)

    by_block = []
    for p in range(2):
        g_ref[...] = outer[p]
        v_ref[p] = by_group([g_ref[pl.ds(j, EX * KP // 4, stride=4), :] for j in range(4)])
        by_block.append(by_group([outer[p][e * KP:(e + 1) * KP] for e in range(EX)]))

    table = split(jnp.concatenate(by_block, axis=0))
    picked = sum(lax.dot_general(onehot, v, TN, preferred_element_type=jnp.float32) for v in table)
    for e in range(EX):
        r = [[jnp.broadcast_to(v_ref[p, pl.ds(2 * y + h + 8 * e, 1), :], (n_dp, 128)) for h in range(2)] for p in range(2)]
        send_d[:, e, :] = jnp.where(is_up, jnp.where(far_half, r[1][1], r[1][0]), jnp.where(far_half, r[0][1], r[0][0]))
    send_d[:, EX, :] = picked

    def d_send(k):
        who = lax.rem(at + k % PLANE, PLANE)
        half_, line_ = on_ring(z + reach(core, k // PLANE))
        dst = line_ * PLANE + who
        pltpu.make_async_remote_copy(
            src_ref=send_d.at[dst, pl.ds(0, EX + 1)], dst_ref=recv_d.at[held, pl.ds(0, EX + 1)],
            send_sem=sd_sem, recv_sem=rd_sem, device_id={"dp": dst, "tensor": y * 2 + half_}, device_id_type=MESH,
        ).start()

    pl.semaphore_wait(known_sem, 2)

    def hops(k):
        return min(k // PLANE, runs - k // PLANE) + min(k % PLANE, PLANE - k % PLANE) // 2

    owner_half, _ = on_ring(z + mid)
    for p in range(2):
        ev_s[p] = v_ref[p, pl.ds(2 * y + owner_half, EX, stride=8), :]
    ev_copy = pltpu.make_async_remote_copy(
        src_ref=ev_s, dst_ref=ev_r, send_sem=ev_sem.at[0], recv_sem=ev_sem.at[1], device_id=ring_peer(mid), device_id_type=MESH,
    )
    ev_copy.start()

    for k in sorted(range(1, n_dp), key=hops, reverse=True):
        d_send(k)
    recv_d[held] = send_d[d]
    for i in range(YN):
        @pl.when(y != i)
        def _():
            for h in range(2):
                y_send(i, h).wait_send()
    seg_copy.wait_send()
    for c in swaps[0] + swaps[1] + gathers:
        c.wait_send()
    whole = pltpu.make_async_remote_copy(
        src_ref=send_d.at[pl.ds(0, n_dp - 1), pl.ds(0, EX + 1)], dst_ref=recv_d.at[pl.ds(0, n_dp - 1), pl.ds(0, EX + 1)],
        send_sem=sd_sem, recv_sem=rd_sem, device_id=ring_peer(mid), device_id_type=MESH,
    )
    whole.wait_recv()
    rows_t = recv_d[:, EX, :].T
    left = jnp.concatenate([rows_t[e * KP:(e + 1) * KP] for e in range(EX)], axis=1)
    right = jnp.concatenate([recv_d[:, e, :] for e in range(EX)], axis=0)
    fisher = dot3(split(left), split(right), (((1,), (0,)), ((), ())))
    f_ref[0] = fisher * (1.0 / EXAMPLES)
    ev_copy.wait()
    ev_ref[...] = ev_r[...]
    whole.wait_send()


def hand_over(ev_ref, f_ref, ev_out, f_out, sem):
    copies = [pltpu.make_async_copy(ev_ref, ev_out, sem.at[0]), pltpu.make_async_copy(f_ref, f_out, sem.at[1])]
    for c in copies:
        c.start()
    for c in copies:
        c.wait()


def shards(xo, go, xu, gu, pxo, pgo, pxu, pgu, seg, owner):
    n_dp = lax.axis_size("dp")
    k1, k2 = xo.shape[1], gu.shape[1]
    bf, f32, i32 = jnp.bfloat16, jnp.float32, jnp.int32
    hbm, vmem = pl.BlockSpec(memory_space=pltpu.HBM), pl.BlockSpec(memory_space=pltpu.VMEM)
    dma, vm = pltpu.SemaphoreType.DMA, pltpu.VMEM
    outs = (jax.ShapeDtypeStruct((2, EX, 128), f32), jax.ShapeDtypeStruct((1, KP, 128), f32))
    args = (xo, go, xu, gu, pxo.T, pgo.T, pxu.T, pgu.T, seg, owner.reshape(1, -1))
    ev, fisher = pl.pallas_call(
        functools.partial(kernel, n_dp),
        out_shape=outs,
        in_specs=[hbm] * 10,
        out_specs=(vmem, vmem),
        scratch_shapes=[
            vm((TOK, k1), bf), vm((TOK, k1), bf), vm((TOK, k1), bf), vm((TOK, k2), bf),
            vm((KP, k1), bf), vm((KP, k1), bf), vm((KP, k1), bf), vm((KP, k2), bf),
            vm((1, TOK), i32), vm((1, owner.shape[0]), i32), vm((2, EX, 128), f32), vm((2, EX, 128), f32),
            vm((4, 2, KP, TOK // 2), f32), vm((YN, 2, KP, TOK // 2), f32), vm((1, TOK), i32), vm((2, KP, TOK // 2), f32), vm((2, 2, KP, TOK // 2), f32),
            vm((4, 2, KP, TOK // 2), f32), vm((128, 128), f32), vm((2, KP, 128), f32), vm((n_dp, 8, 128), f32), vm((n_dp, 8, 128), f32),
            dma((11,)), dma((4, 2)), dma((4, 2)), dma((2,)), dma((2, 2)), dma((2, 2)), dma((3, 2)), dma((4, 2)), dma((2,)), dma, dma,
            pltpu.SemaphoreType.REGULAR, pltpu.SemaphoreType.REGULAR,
        ],
        compiler_params=pltpu.CompilerParams(collective_id=0, has_side_effects=True, vmem_limit_bytes=32 << 20),
    )(*(pltpu.with_memory_space_constraint(a, pltpu.HBM) for a in args))
    return pl.pallas_call(
        hand_over, out_shape=outs, in_specs=[vmem, vmem], out_specs=(hbm, hbm), scratch_shapes=[dma((2,))],
        compiler_params=pltpu.CompilerParams(vmem_limit_bytes=4 << 20),
    )(ev, fisher)


def solution(mesh):
    in_specs = (P("dp", "tensor"),) * 4 + (P("tensor", None),) * 4 + (P("dp", None), P())
    out_specs = (P(None, "dp", "tensor"), P("dp", None, "tensor"))
    return jax.shard_map(shards, mesh=mesh, in_specs=in_specs, out_specs=out_specs, check_vma=False)
```

```python
import functools

import jax
import jax.numpy as jnp
from jax import lax
from jax.experimental import pallas as pl
from jax.experimental.pallas import tpu as pltpu
from jax.sharding import PartitionSpec as P

TOK = 256
EX = 4
KP = 32
BLOCKS = 64
EXAMPLES = 256
YN = 4
PLANE = 8
MESH = pl.DeviceIdType.MESH
NT = (((1,), (1,)), ((), ()))
TN = (((0,), (0,)), ((), ()))


def split(x):
    top = x.astype(jnp.bfloat16)
    return top, (x - top.astype(jnp.float32)).astype(jnp.bfloat16)


def dot3(a, b, dims):
    (a1, a2), (b1, b2) = a, b

    def one(p, q):
        return lax.dot_general(p, q, dims, preferred_element_type=jnp.float32)

    return one(a1, b1) + (one(a1, b2) + one(a2, b1))


def kernel(
    n_dp,
    xo_ref, go_ref, xu_ref, gu_ref, pxo_ref, pgo_ref, pxu_ref, pgu_ref, seg_ref, own_ref,
    ev_ref, f_ref,
    xo, go, xu, gu, pxo, pgo, pxu, pgu, seg_v, own_v, ev_s, ev_r,
    part, recv_y, seg_r, sum_z, recv_z, full, g_ref, v_ref, send_d, recv_d,
    in_sem, sy_sem, ry_sem, seg_sem, sz_sem, rz_sem, sg_sem, rg_sem, ev_sem, sd_sem, rd_sem, met_sem, known_sem,
):
    d = lax.axis_index("dp")
    t = lax.axis_index("tensor")
    y, zh = t // 2, lax.rem(t, 2)
    plane = d // PLANE
    at, core = lax.rem(d, PLANE), lax.rem(d, 2)
    runs = n_dp // PLANE
    ring = 2 * runs
    mid = runs // 2
    z = zh * runs + plane
    held = lax.rem(z + mid, runs) * PLANE + at

    def on_ring(pos):
        pos = lax.rem(pos + ring, ring)
        return pos // runs, lax.rem(pos, runs)

    def ring_peer(step):
        half, line = on_ring(z + step)
        return {"dp": line * PLANE + at, "tensor": y * 2 + half}

    def y_peer(j):
        return lax.rem(y + j, YN)

    def reach(of_core, r):
        low = mid - 1 + of_core
        return lax.rem(r + low, runs) - low

    half = TOK // 2
    loads = [
        (pxo_ref, pxo), (xo_ref, xo), (pgo_ref, pgo), (go_ref, go), (pxu_ref, pxu), (xu_ref, xu), (pgu_ref, pgu),
        (gu_ref.at[pl.ds(0, half)], gu.at[pl.ds(0, half)]), (gu_ref.at[pl.ds(half, half)], gu.at[pl.ds(half, half)]),
        (seg_ref, seg_v), (own_ref, own_v),
    ]
    copies = [pltpu.make_async_copy(s, dst, in_sem.at[i]) for i, (s, dst) in enumerate(loads)]
    for c in copies:
        c.start()

    barrier = pltpu.get_barrier_semaphore()
    near = (2, -2, 1, -1)
    for j in (2, 1, 3):
        pl.semaphore_signal(barrier, inc=1, device_id={"tensor": y_peer(j) * 2 + zh}, device_id_type=MESH)
    for k in (4, 5, 3, 2, 6, 7, 1):
        pl.semaphore_signal(barrier, inc=1, device_id={"dp": plane * PLANE + lax.rem(at + k, PLANE)}, device_id_type=MESH)
    for step in near:
        pl.semaphore_signal(barrier, inc=1, device_id=ring_peer(step), device_id_type=MESH)

    def project(w, x):
        return lax.dot_general(w, x, NT, preferred_element_type=jnp.float32)

    def y_send(i, h):
        return pltpu.make_async_remote_copy(
            src_ref=part.at[i, h], dst_ref=recv_y.at[y, h], send_sem=sy_sem.at[i, h], recv_sem=ry_sem.at[y, h],
            device_id={"tensor": i * 2 + zh}, device_id_type=MESH,
        )

    def y_start(i, h):
        @pl.when(y != i)
        def _():
            y_send(i, h).start()

    for i, (w, x) in enumerate(((pxo, xo), (pgo, go), (pxu, xu))):
        copies[2 * i].wait()
        copies[2 * i + 1].wait()
        q = project(w[...], x[...])
        part[i, 0] = q[:, :half]
        part[i, 1] = q[:, half:]
    pl.semaphore_wait(barrier, PLANE - 1 + len(near) + YN - 1)
    for h in range(2):
        for i in range(3):
            y_start(i, h)
    for step in near:
        pl.semaphore_signal(met_sem, inc=1, device_id=ring_peer(step), device_id_type=MESH)
    copies[6].wait()
    for h in range(2):
        copies[7 + h].wait()
        part[3, h] = project(pgu[...], gu[pl.ds(h * half, half), :])
        y_start(3, h)
    copies[9].wait()
    copies[10].wait()

    swaps = []
    for h in range(2):
        total = part[y, h]
        for j in range(1, YN):
            p = y_peer(j)
            pltpu.make_async_remote_copy(
                src_ref=part.at[p, h], dst_ref=recv_y.at[p, h], send_sem=sy_sem.at[p, h], recv_sem=ry_sem.at[p, h],
                device_id={"tensor": p * 2 + zh}, device_id_type=MESH,
            ).wait_recv()
            total += recv_y[p, h]
        sum_z[h] = total
        if h == 0:
            pl.semaphore_wait(met_sem, len(near))
        swaps.append([
            pltpu.make_async_remote_copy(
                src_ref=sum_z.at[h], dst_ref=recv_z.at[i, h], send_sem=sz_sem.at[i, h], recv_sem=rz_sem.at[i, h],
                device_id=ring_peer(step), device_id_type=MESH,
            )
            for i, step in enumerate((mid, -mid))
        ])
        for c in swaps[h]:
            c.start()
    for step in near[:2]:
        pl.semaphore_signal(known_sem, inc=1, device_id=ring_peer(step), device_id_type=MESH)
    seg_copy = pltpu.make_async_remote_copy(
        src_ref=seg_v, dst_ref=seg_r, send_sem=seg_sem.at[0], recv_sem=seg_sem.at[1], device_id=ring_peer(mid), device_id_type=MESH,
    )
    seg_copy.start()
    gathers = []
    for h in range(2):
        for c in swaps[h]:
            c.wait_recv()
        full[y, h] = recv_z[0, h] + recv_z[1, h]
        for j in (2, 1, 3):
            p = y_peer(j)
            c = pltpu.make_async_remote_copy(
                src_ref=full.at[y, h], dst_ref=full.at[y, h], send_sem=sg_sem.at[j - 1, h], recv_sem=rg_sem.at[y, h],
                device_id={"tensor": p * 2 + zh}, device_id_type=MESH,
            )
            c.start()
            gathers.append(c)
    seg_copy.wait_recv()
    seg = seg_r[...]
    scale = (EX / TOK) ** 0.5
    masks = [jnp.where(seg == e, scale, 0.0).astype(jnp.bfloat16) for e in range(EX)]
    onehot = (lax.broadcasted_iota(jnp.int32, (BLOCKS, n_dp), 0) == own_v[...]).astype(jnp.bfloat16)
    block_is_up = (lax.broadcasted_iota(jnp.int32, (BLOCKS, 128), 0) >= KP).astype(jnp.bfloat16)
    is_up = lax.dot_general(onehot, block_is_up, TN, preferred_element_type=jnp.float32) > 0.5
    low = mid - 1 + core
    line = lax.broadcasted_iota(jnp.int32, (n_dp, 128), 0) // PLANE
    pos = z + lax.rem(line - z + low + ring, runs) - low
    far_half = lax.rem(pos + ring, ring) >= runs
    group = lax.broadcasted_iota(jnp.int32, (EX * KP // 4, 128), 1) // KP

    def by_group(rows):
        return jnp.where(group == 0, rows[0], jnp.where(group == 1, rows[1], jnp.where(group == 2, rows[2], rows[3])))

    outer = [0.0, 0.0]
    for h in range(2):
        for j in range(1, YN):
            p = y_peer(j)
            pltpu.make_async_remote_copy(
                src_ref=full.at[p, h], dst_ref=full.at[p, h], send_sem=sg_sem.at[j - 1, h], recv_sem=rg_sem.at[p, h],
                device_id={"tensor": p * 2 + zh}, device_id_type=MESH,
            ).wait_recv()
        m_h = [m[:, h * half:(h + 1) * half] for m in masks]
        for p in range(2):
            low, high = split(full[2 * p, h]), split(full[2 * p + 1, h])
            low_4 = [jnp.concatenate([v] * 4, axis=0) for v in low]
            high_e = [jnp.concatenate([v * m for m in m_h], axis=0) for v in high]
            outer[p] += dot3(high_e, low_4, NT)

    by_block = []
    for p in range(2):
        g_ref[...] = outer[p]
        v_ref[p] = by_group([g_ref[pl.ds(j, EX * KP // 4, stride=4), :] for j in range(4)])
        by_block.append(by_group([outer[p][e * KP:(e + 1) * KP] for e in range(EX)]))

    table = split(jnp.concatenate(by_block, axis=0))
    picked = sum(lax.dot_general(onehot, v, TN, preferred_element_type=jnp.float32) for v in table)
    for e in range(EX):
        r = [[jnp.broadcast_to(v_ref[p, pl.ds(2 * y + h + 8 * e, 1), :], (n_dp, 128)) for h in range(2)] for p in range(2)]
        send_d[:, e, :] = jnp.where(is_up, jnp.where(far_half, r[1][1], r[1][0]), jnp.where(far_half, r[0][1], r[0][0]))
    send_d[:, EX, :] = picked

    def d_send(k):
        who = lax.rem(at + k % PLANE, PLANE)
        half_, line_ = on_ring(z + reach(core, k // PLANE))
        dst = line_ * PLANE + who
        pltpu.make_async_remote_copy(
            src_ref=send_d.at[dst, pl.ds(0, EX + 1)], dst_ref=recv_d.at[held, pl.ds(0, EX + 1)],
            send_sem=sd_sem, recv_sem=rd_sem, device_id={"dp": dst, "tensor": y * 2 + half_}, device_id_type=MESH,
        ).start()

    pl.semaphore_wait(known_sem, 2)

    def hops(k):
        return min(k // PLANE, runs - k // PLANE) + min(k % PLANE, PLANE - k % PLANE) // 2

    for k in sorted(range(1, n_dp), key=hops, reverse=True):
        d_send(k)
    recv_d[held] = send_d[d]
    owner_half, _ = on_ring(z + mid)
    for p in range(2):
        ev_s[p] = v_ref[p, pl.ds(2 * y + owner_half, EX, stride=8), :]
    ev_copy = pltpu.make_async_remote_copy(
        src_ref=ev_s, dst_ref=ev_r, send_sem=ev_sem.at[0], recv_sem=ev_sem.at[1], device_id=ring_peer(mid), device_id_type=MESH,
    )
    ev_copy.start()
    for i in range(YN):
        @pl.when(y != i)
        def _():
            for h in range(2):
                y_send(i, h).wait_send()
    seg_copy.wait_send()
    for c in swaps[0] + swaps[1] + gathers:
        c.wait_send()
    whole = pltpu.make_async_remote_copy(
        src_ref=send_d.at[pl.ds(0, n_dp - 1), pl.ds(0, EX + 1)], dst_ref=recv_d.at[pl.ds(0, n_dp - 1), pl.ds(0, EX + 1)],
        send_sem=sd_sem, recv_sem=rd_sem, device_id=ring_peer(mid), device_id_type=MESH,
    )
    whole.wait_recv()
    rows_t = recv_d[:, EX, :].T
    left = jnp.concatenate([rows_t[e * KP:(e + 1) * KP] for e in range(EX)], axis=1)
    right = jnp.concatenate([recv_d[:, e, :] for e in range(EX)], axis=0)
    fisher = dot3(split(left), split(right), (((1,), (0,)), ((), ())))
    f_ref[0] = fisher * (1.0 / EXAMPLES)
    ev_copy.wait()
    ev_ref[...] = ev_r[...]
    whole.wait_send()


def hand_over(ev_ref, f_ref, ev_out, f_out, sem):
    copies = [pltpu.make_async_copy(ev_ref, ev_out, sem.at[0]), pltpu.make_async_copy(f_ref, f_out, sem.at[1])]
    for c in copies:
        c.start()
    for c in copies:
        c.wait()


def shards(xo, go, xu, gu, pxo, pgo, pxu, pgu, seg, owner):
    n_dp = lax.axis_size("dp")
    k1, k2 = xo.shape[1], gu.shape[1]
    bf, f32, i32 = jnp.bfloat16, jnp.float32, jnp.int32
    hbm, vmem = pl.BlockSpec(memory_space=pltpu.HBM), pl.BlockSpec(memory_space=pltpu.VMEM)
    dma, vm = pltpu.SemaphoreType.DMA, pltpu.VMEM
    outs = (jax.ShapeDtypeStruct((2, EX, 128), f32), jax.ShapeDtypeStruct((1, KP, 128), f32))
    args = (xo, go, xu, gu, pxo.T, pgo.T, pxu.T, pgu.T, seg, owner.reshape(1, -1))
    ev, fisher = pl.pallas_call(
        functools.partial(kernel, n_dp),
        out_shape=outs,
        in_specs=[hbm] * 10,
        out_specs=(vmem, vmem),
        scratch_shapes=[
            vm((TOK, k1), bf), vm((TOK, k1), bf), vm((TOK, k1), bf), vm((TOK, k2), bf),
            vm((KP, k1), bf), vm((KP, k1), bf), vm((KP, k1), bf), vm((KP, k2), bf),
            vm((1, TOK), i32), vm((1, owner.shape[0]), i32), vm((2, EX, 128), f32), vm((2, EX, 128), f32),
            vm((4, 2, KP, TOK // 2), f32), vm((YN, 2, KP, TOK // 2), f32), vm((1, TOK), i32), vm((2, KP, TOK // 2), f32), vm((2, 2, KP, TOK // 2), f32),
            vm((4, 2, KP, TOK // 2), f32), vm((128, 128), f32), vm((2, KP, 128), f32), vm((n_dp, 8, 128), f32), vm((n_dp, 8, 128), f32),
            dma((11,)), dma((4, 2)), dma((4, 2)), dma((2,)), dma((2, 2)), dma((2, 2)), dma((3, 2)), dma((4, 2)), dma((2,)), dma, dma,
            pltpu.SemaphoreType.REGULAR, pltpu.SemaphoreType.REGULAR,
        ],
        compiler_params=pltpu.CompilerParams(collective_id=0, has_side_effects=True, vmem_limit_bytes=32 << 20),
    )(*(pltpu.with_memory_space_constraint(a, pltpu.HBM) for a in args))
    return pl.pallas_call(
        hand_over, out_shape=outs, in_specs=[vmem, vmem], out_specs=(hbm, hbm), scratch_shapes=[dma((2,))],
        compiler_params=pltpu.CompilerParams(vmem_limit_bytes=4 << 20),
    )(ev, fisher)


def solution(mesh):
    in_specs = (P("dp", "tensor"),) * 4 + (P("tensor", None),) * 4 + (P("dp", None), P())
    out_specs = (P(None, "dp", "tensor"), P("dp", None, "tensor"))
    return jax.shard_map(shards, mesh=mesh, in_specs=in_specs, out_specs=out_specs, check_vma=False)
```

```python
import functools

import jax
import jax.numpy as jnp
from jax import lax
from jax.experimental import pallas as pl
from jax.experimental.pallas import tpu as pltpu
from jax.sharding import PartitionSpec as P

TOK = 256
EX = 4
KP = 32
BLOCKS = 64
EXAMPLES = 256
YN = 4
PLANE = 8
MESH = pl.DeviceIdType.MESH
NT = (((1,), (1,)), ((), ()))
TN = (((0,), (0,)), ((), ()))


def split(x):
    top = x.astype(jnp.bfloat16)
    return top, (x - top.astype(jnp.float32)).astype(jnp.bfloat16)


def dot3(a, b, dims):
    (a1, a2), (b1, b2) = a, b

    def one(p, q):
        return lax.dot_general(p, q, dims, preferred_element_type=jnp.float32)

    return one(a1, b1) + (one(a1, b2) + one(a2, b1))


def kernel(
    n_dp,
    xo_ref, go_ref, xu_ref, gu_ref, pxo_ref, pgo_ref, pxu_ref, pgu_ref, seg_ref, own_ref,
    ev_ref, f_ref,
    xo, go, xu, gu, pxo, pgo, pxu, pgu, seg_v, own_v, ev_s, ev_r,
    part, recv_y, seg_r, sum_z, recv_z, full, g_ref, v_ref, send_d, recv_d,
    in_sem, sy_sem, ry_sem, seg_sem, sz_sem, rz_sem, sg_sem, rg_sem, ev_sem, sd_sem, rd_sem, met_sem, known_sem,
):
    d = lax.axis_index("dp")
    t = lax.axis_index("tensor")
    y, zh = t // 2, lax.rem(t, 2)
    plane = d // PLANE
    at, core = lax.rem(d, PLANE), lax.rem(d, 2)
    runs = n_dp // PLANE
    ring = 2 * runs
    mid = runs // 2
    z = zh * runs + plane
    held = lax.rem(z + mid, runs) * PLANE + at

    def on_ring(pos):
        pos = lax.rem(pos + ring, ring)
        return pos // runs, lax.rem(pos, runs)

    def ring_peer(step):
        half, line = on_ring(z + step)
        return {"dp": line * PLANE + at, "tensor": y * 2 + half}

    def y_peer(j):
        return lax.rem(y + j, YN)

    def reach(of_core, r):
        low = mid - 1 + of_core
        return lax.rem(r + low, runs) - low

    half = TOK // 2
    loads = [
        (pxo_ref, pxo), (xo_ref, xo), (pgo_ref, pgo), (go_ref, go), (pxu_ref, pxu), (xu_ref, xu), (pgu_ref, pgu),
        (gu_ref.at[pl.ds(0, half)], gu.at[pl.ds(0, half)]), (gu_ref.at[pl.ds(half, half)], gu.at[pl.ds(half, half)]),
        (seg_ref, seg_v), (own_ref, own_v),
    ]
    copies = [pltpu.make_async_copy(s, dst, in_sem.at[i]) for i, (s, dst) in enumerate(loads)]
    for c in copies:
        c.start()

    barrier = pltpu.get_barrier_semaphore()
    near = (2, -2, 1, -1)
    for j in (2, 1, 3):
        pl.semaphore_signal(barrier, inc=1, device_id={"tensor": y_peer(j) * 2 + zh}, device_id_type=MESH)
    for k in (4, 5, 3, 2, 6, 7, 1):
        pl.semaphore_signal(barrier, inc=1, device_id={"dp": plane * PLANE + lax.rem(at + k, PLANE)}, device_id_type=MESH)
    for step in near:
        pl.semaphore_signal(barrier, inc=1, device_id=ring_peer(step), device_id_type=MESH)

    def project(w, x):
        return lax.dot_general(w, x, NT, preferred_element_type=jnp.float32)

    def y_send(i, h):
        return pltpu.make_async_remote_copy(
            src_ref=part.at[i, h], dst_ref=recv_y.at[y, h], send_sem=sy_sem.at[i, h], recv_sem=ry_sem.at[y, h],
            device_id={"tensor": i * 2 + zh}, device_id_type=MESH,
        )

    def y_start(i, h):
        @pl.when(y != i)
        def _():
            y_send(i, h).start()

    for i, (w, x) in enumerate(((pxo, xo), (pgo, go), (pxu, xu))):
        copies[2 * i].wait()
        copies[2 * i + 1].wait()
        q = project(w[...], x[...])
        part[i, 0] = q[:, :half]
        part[i, 1] = q[:, half:]
    pl.semaphore_wait(barrier, PLANE - 1 + len(near) + YN - 1)
    for h in range(2):
        for i in range(3):
            y_start(i, h)
    for step in near:
        pl.semaphore_signal(met_sem, inc=1, device_id=ring_peer(step), device_id_type=MESH)
    copies[6].wait()
    for h in range(2):
        copies[7 + h].wait()
        part[3, h] = project(pgu[...], gu[pl.ds(h * half, half), :])
        y_start(3, h)
    copies[9].wait()
    copies[10].wait()

    seg_copy = pltpu.make_async_remote_copy(
        src_ref=seg_v, dst_ref=seg_r, send_sem=seg_sem.at[0], recv_sem=seg_sem.at[1], device_id=ring_peer(mid), device_id_type=MESH,
    )
    swaps = []
    for h in range(2):
        total = part[y, h]
        for j in range(1, YN):
            p = y_peer(j)
            pltpu.make_async_remote_copy(
                src_ref=part.at[p, h], dst_ref=recv_y.at[p, h], send_sem=sy_sem.at[p, h], recv_sem=ry_sem.at[p, h],
                device_id={"tensor": p * 2 + zh}, device_id_type=MESH,
            ).wait_recv()
            total += recv_y[p, h]
        sum_z[h] = total
        if h == 0:
            pl.semaphore_wait(met_sem, len(near))
        swaps.append([
            pltpu.make_async_remote_copy(
                src_ref=sum_z.at[h], dst_ref=recv_z.at[i, h], send_sem=sz_sem.at[i, h], recv_sem=rz_sem.at[i, h],
                device_id=ring_peer(mid * (1 - 2 * i)), device_id_type=MESH,
            )
            for i in (core, 1 - core)
        ])
        for c in swaps[h]:
            c.start()
        if h == 0:
            seg_copy.start()
    for step in near[:2]:
        pl.semaphore_signal(known_sem, inc=1, device_id=ring_peer(step), device_id_type=MESH)
    gathers = []
    for h in range(2):
        for c in swaps[h]:
            c.wait_recv()
        full[y, h] = recv_z[0, h] + recv_z[1, h]
        for j in (2, 1, 3):
            p = y_peer(j)
            c = pltpu.make_async_remote_copy(
                src_ref=full.at[y, h], dst_ref=full.at[y, h], send_sem=sg_sem.at[j - 1, h], recv_sem=rg_sem.at[y, h],
                device_id={"tensor": p * 2 + zh}, device_id_type=MESH,
            )
            c.start()
            gathers.append(c)
    seg_copy.wait_recv()
    seg = seg_r[...]
    scale = (EX / TOK) ** 0.5
    masks = [jnp.where(seg == e, scale, 0.0).astype(jnp.bfloat16) for e in range(EX)]
    onehot = (lax.broadcasted_iota(jnp.int32, (BLOCKS, n_dp), 0) == own_v[...]).astype(jnp.bfloat16)
    block_is_up = (lax.broadcasted_iota(jnp.int32, (BLOCKS, 128), 0) >= KP).astype(jnp.bfloat16)
    is_up = lax.dot_general(onehot, block_is_up, TN, preferred_element_type=jnp.float32) > 0.5
    low = mid - 1 + core
    line = lax.broadcasted_iota(jnp.int32, (n_dp, 128), 0) // PLANE
    pos = z + lax.rem(line - z + low + ring, runs) - low
    far_half = lax.rem(pos + ring, ring) >= runs
    group = lax.broadcasted_iota(jnp.int32, (EX * KP // 4, 128), 1) // KP

    def by_group(rows):
        return jnp.where(group == 0, rows[0], jnp.where(group == 1, rows[1], jnp.where(group == 2, rows[2], rows[3])))

    outer = [0.0, 0.0]
    for h in range(2):
        for j in range(1, YN):
            p = y_peer(j)
            pltpu.make_async_remote_copy(
                src_ref=full.at[p, h], dst_ref=full.at[p, h], send_sem=sg_sem.at[j - 1, h], recv_sem=rg_sem.at[p, h],
                device_id={"tensor": p * 2 + zh}, device_id_type=MESH,
            ).wait_recv()
        m_h = [m[:, h * half:(h + 1) * half] for m in masks]
        for p in range(2):
            low, high = split(full[2 * p, h]), split(full[2 * p + 1, h])
            low_4 = [jnp.concatenate([v] * 4, axis=0) for v in low]
            high_e = [jnp.concatenate([v * m for m in m_h], axis=0) for v in high]
            outer[p] += dot3(high_e, low_4, NT)

    by_block = []
    for p in range(2):
        g_ref[...] = outer[p]
        v_ref[p] = by_group([g_ref[pl.ds(j, EX * KP // 4, stride=4), :] for j in range(4)])
        by_block.append(by_group([outer[p][e * KP:(e + 1) * KP] for e in range(EX)]))

    table = split(jnp.concatenate(by_block, axis=0))
    picked = sum(lax.dot_general(onehot, v, TN, preferred_element_type=jnp.float32) for v in table)
    for e in range(EX):
        r = [[jnp.broadcast_to(v_ref[p, pl.ds(2 * y + h + 8 * e, 1), :], (n_dp, 128)) for h in range(2)] for p in range(2)]
        send_d[:, e, :] = jnp.where(is_up, jnp.where(far_half, r[1][1], r[1][0]), jnp.where(far_half, r[0][1], r[0][0]))
    send_d[:, EX, :] = picked

    def d_send(k):
        who = lax.rem(at + k % PLANE, PLANE)
        half_, line_ = on_ring(z + reach(core, k // PLANE))
        dst = line_ * PLANE + who
        pltpu.make_async_remote_copy(
            src_ref=send_d.at[dst, pl.ds(0, EX + 1)], dst_ref=recv_d.at[held, pl.ds(0, EX + 1)],
            send_sem=sd_sem, recv_sem=rd_sem, device_id={"dp": dst, "tensor": y * 2 + half_}, device_id_type=MESH,
        ).start()

    pl.semaphore_wait(known_sem, 2)

    def hops(k):
        return min(k // PLANE, runs - k // PLANE) + min(k % PLANE, PLANE - k % PLANE) // 2

    for k in sorted(range(1, n_dp), key=hops, reverse=True):
        d_send(k)
    recv_d[held] = send_d[d]
    owner_half, _ = on_ring(z + mid)
    for p in range(2):
        ev_s[p] = v_ref[p, pl.ds(2 * y + owner_half, EX, stride=8), :]
    ev_copy = pltpu.make_async_remote_copy(
        src_ref=ev_s, dst_ref=ev_r, send_sem=ev_sem.at[0], recv_sem=ev_sem.at[1], device_id=ring_peer(mid), device_id_type=MESH,
    )
    ev_copy.start()
    for i in range(YN):
        @pl.when(y != i)
        def _():
            for h in range(2):
                y_send(i, h).wait_send()
    seg_copy.wait_send()
    for c in swaps[0] + swaps[1] + gathers:
        c.wait_send()
    whole = pltpu.make_async_remote_copy(
        src_ref=send_d.at[pl.ds(0, n_dp - 1), pl.ds(0, EX + 1)], dst_ref=recv_d.at[pl.ds(0, n_dp - 1), pl.ds(0, EX + 1)],
        send_sem=sd_sem, recv_sem=rd_sem, device_id=ring_peer(mid), device_id_type=MESH,
    )
    whole.wait_recv()
    rows_t = recv_d[:, EX, :].T
    left = jnp.concatenate([rows_t[e * KP:(e + 1) * KP] for e in range(EX)], axis=1)
    right = jnp.concatenate([recv_d[:, e, :] for e in range(EX)], axis=0)
    fisher = dot3(split(left), split(right), (((1,), (0,)), ((), ())))
    f_ref[0] = fisher * (1.0 / EXAMPLES)
    ev_copy.wait()
    ev_ref[...] = ev_r[...]
    whole.wait_send()


def hand_over(ev_ref, f_ref, ev_out, f_out, sem):
    copies = [pltpu.make_async_copy(ev_ref, ev_out, sem.at[0]), pltpu.make_async_copy(f_ref, f_out, sem.at[1])]
    for c in copies:
        c.start()
    for c in copies:
        c.wait()


def shards(xo, go, xu, gu, pxo, pgo, pxu, pgu, seg, owner):
    n_dp = lax.axis_size("dp")
    k1, k2 = xo.shape[1], gu.shape[1]
    bf, f32, i32 = jnp.bfloat16, jnp.float32, jnp.int32
    hbm, vmem = pl.BlockSpec(memory_space=pltpu.HBM), pl.BlockSpec(memory_space=pltpu.VMEM)
    dma, vm = pltpu.SemaphoreType.DMA, pltpu.VMEM
    outs = (jax.ShapeDtypeStruct((2, EX, 128), f32), jax.ShapeDtypeStruct((1, KP, 128), f32))
    args = (xo, go, xu, gu, pxo.T, pgo.T, pxu.T, pgu.T, seg, owner.reshape(1, -1))
    ev, fisher = pl.pallas_call(
        functools.partial(kernel, n_dp),
        out_shape=outs,
        in_specs=[hbm] * 10,
        out_specs=(vmem, vmem),
        scratch_shapes=[
            vm((TOK, k1), bf), vm((TOK, k1), bf), vm((TOK, k1), bf), vm((TOK, k2), bf),
            vm((KP, k1), bf), vm((KP, k1), bf), vm((KP, k1), bf), vm((KP, k2), bf),
            vm((1, TOK), i32), vm((1, owner.shape[0]), i32), vm((2, EX, 128), f32), vm((2, EX, 128), f32),
            vm((4, 2, KP, TOK // 2), f32), vm((YN, 2, KP, TOK // 2), f32), vm((1, TOK), i32), vm((2, KP, TOK // 2), f32), vm((2, 2, KP, TOK // 2), f32),
            vm((4, 2, KP, TOK // 2), f32), vm((128, 128), f32), vm((2, KP, 128), f32), vm((n_dp, 8, 128), f32), vm((n_dp, 8, 128), f32),
            dma((11,)), dma((4, 2)), dma((4, 2)), dma((2,)), dma((2, 2)), dma((2, 2)), dma((3, 2)), dma((4, 2)), dma((2,)), dma, dma,
            pltpu.SemaphoreType.REGULAR, pltpu.SemaphoreType.REGULAR,
        ],
        compiler_params=pltpu.CompilerParams(collective_id=0, has_side_effects=True, vmem_limit_bytes=32 << 20),
    )(*(pltpu.with_memory_space_constraint(a, pltpu.HBM) for a in args))
    return pl.pallas_call(
        hand_over, out_shape=outs, in_specs=[vmem, vmem], out_specs=(hbm, hbm), scratch_shapes=[dma((2,))],
        compiler_params=pltpu.CompilerParams(vmem_limit_bytes=4 << 20),
    )(ev, fisher)


def solution(mesh):
    in_specs = (P("dp", "tensor"),) * 4 + (P("tensor", None),) * 4 + (P("dp", None), P())
    out_specs = (P(None, "dp", "tensor"), P("dp", None, "tensor"))
    return jax.shard_map(shards, mesh=mesh, in_specs=in_specs, out_specs=out_specs, check_vma=False)
```
